512 devices in a mesh: layer: 4 (over z_hi), facet: 128 (over y, z_lo, x, core).
Axes of the slice: x: 4, y: 8, z: 8 (z_hi: 4, z_lo: 2; z = z_hi * 2 + z_lo), core: 2. Of those that a mesh axis runs over, the one named last changes fastest.
Arguments:
- model_strip: bfloat16 [128, 2, 64, 8192], P('facet', None, None, 'layer'), may hold values from -6 to 6
- screen_angle: bfloat16 [4, 128, 64, 8192], P('layer', 'facet'), may hold values from -3.140625 to 3.140625
- facet_window: float32 [128, 8192], P('facet'), may hold values from 0.04 to 0.16
- facet_shift: int32 [128], P('facet'), may hold values from 0 to 8191
- kernel_taps: float32 [7], replicated, may hold values from 0.2 to 0.6
- plane_angle: float32 [4, 8], P('layer'), may hold values from -3.140625 to 3.140625
- u_cell: int32 [4, 128, 512], P('layer', 'facet'), may hold values from 0 to 63
- v_cell: int32 [4, 128, 512], P('layer', 'facet'), may hold values from 0 to 63
- w_plane: int32 [4, 128, 512], P('layer', 'facet'), may hold values from 0 to 7
- observed: float32 [4, 128, 2, 512], P('layer', 'facet'), may hold values from -6 to 6
Outputs:
- residual: float32 [4, 128, 2, 512], P('layer', 'facet')
- gradient: float32 [128, 2, 64, 8192], P('facet', None, None, 'layer')
The draws below stay inside these ranges and needn't reach their ends.
All inputs are finite; a program needn't handle non-finite values.
Results may differ from the reference program's by a relative error of at most 0.009.
Values may be sent and summed in bfloat16 or wider, within the bound.
No kernel may reach another device: no remote copies, remote signals or barrier semaphores. Data moves between devices by JAX's collectives and lax.ppermute only.
A program may use at most 64 MiB of HBM per device.

```python
import math
import jax
import jax.numpy as jnp
from jax import lax

STRIP_LEN = 8192
SUB_ROWS = 64
STRIP_COLS = 64
VIS = 512
PLANES = 8
TAPS = 7
SUBGRIDS = 128
LAYERS = 4
FACETS = 128


def touch_ends(entries, rng, low, largest):
    extent = entries.shape
    place = [jax.random.randint(jax.random.fold_in(rng, axis), (), 0, extent[axis]) for axis in range(len(extent))]
    entries = entries.at[tuple(place)].set(low)
    longest = extent.index(max(extent))
    place[longest] = (place[longest] + 1) % extent[longest]
    return entries.at[tuple(place)].set(largest)


def steps_of(stream_key, extent, shards, low, high):
    gain, own = 1.0, jax.random.fold_in(stream_key, 6)
    for dim, shards_of in shards:
        draws = jnp.exp(jax.random.uniform(jax.random.fold_in(own, dim), (shards_of,), jnp.float32, low / len(shards), high / len(shards)))
        gain = gain * jnp.repeat(draws, extent[dim] // shards_of).reshape([-1 if axis == dim else 1 for axis in range(len(extent))])
    return gain


def noise(stream_key, extent, deviation, reach, cuts=(), kind=jnp.bfloat16):
    factor_of = steps_of(stream_key, extent, cuts, -0.22, 0.18) if cuts else 1.0
    array = jax.random.normal(stream_key, extent, jnp.float32) * deviation * factor_of
    return jnp.minimum(jnp.maximum(array, -reach), reach).astype(kind)


def setup_inputs(seed: int = 0) -> dict:
    arg_keys = jax.random.split(jax.random.key(seed), 11)
    return {
        "model_strip": noise(arg_keys[0], (FACETS, 2, STRIP_COLS, STRIP_LEN), 1.0, 6.0, ((0, 128), (3, 4))),
        "screen_angle": jnp.clip(jax.random.uniform(arg_keys[1], (LAYERS, FACETS, STRIP_COLS, STRIP_LEN), jnp.float32, -3.140625, 3.140625), -3.140625, 3.140625).astype(jnp.bfloat16),
        "facet_window": jnp.clip(jnp.exp(math.log(0.16) - 1.3862944 * jax.random.uniform(arg_keys[2], (FACETS, STRIP_LEN), jnp.float32) ** steps_of(arg_keys[2], (FACETS, STRIP_LEN), ((0, 128),), -0.2, 0.2)), 0.04, 0.16),
        "facet_shift": touch_ends(jax.random.randint(arg_keys[3], (FACETS,), 0, STRIP_LEN), jax.random.fold_in(arg_keys[3], 1), 0, STRIP_LEN - 1).astype(jnp.int32),
        "kernel_taps": jnp.clip(jax.random.uniform(arg_keys[4], (TAPS,), jnp.float32, 0.2, 0.6), 0.2, 0.6),
        "plane_angle": jnp.clip(jax.random.uniform(arg_keys[5], (LAYERS, PLANES), jnp.float32, -3.140625, 3.140625), -3.140625, 3.140625),
        "u_cell": touch_ends(jax.random.randint(arg_keys[6], (LAYERS, SUBGRIDS, VIS), 0, SUB_ROWS), jax.random.fold_in(arg_keys[6], 1), 0, SUB_ROWS - 1).astype(jnp.int32),
        "v_cell": touch_ends(jax.random.randint(arg_keys[7], (LAYERS, SUBGRIDS, VIS), 0, STRIP_COLS), jax.random.fold_in(arg_keys[7], 1), 0, STRIP_COLS - 1).astype(jnp.int32),
        "w_plane": touch_ends(jax.random.randint(arg_keys[8], (LAYERS, SUBGRIDS, VIS), 0, PLANES), jax.random.fold_in(arg_keys[8], 1), 0, PLANES - 1).astype(jnp.int32),
        "observed": noise(arg_keys[9], (LAYERS, SUBGRIDS, 2, VIS), 1.0, 6.0, ((0, 4), (1, 128)), jnp.float32),
    }


back_gain = 8.0

def fourier_table(length):
    positions = jnp.arange(length, dtype=jnp.int32)
    turn_count = positions[:, None] * positions[None, :] % length
    angles = 2.0 * math.pi / length * turn_count.astype(jnp.float32)
    norm_scale = 1.0 / math.sqrt(length)
    return (jnp.stack([jnp.cos(angles), -jnp.sin(angles)]) * norm_scale).astype(jnp.bfloat16)

def twiddle():
    low_index = jnp.arange(SUB_ROWS, dtype=jnp.int32)
    high_index = jnp.arange(SUBGRIDS, dtype=jnp.int32)
    turn_count = low_index[:, None] * high_index[None, :] % STRIP_LEN
    angles = 2.0 * math.pi / STRIP_LEN * turn_count.astype(jnp.float32)
    return (jnp.cos(angles), -jnp.sin(angles))

def facet_factor(window, shift_cells):
    positions = jnp.arange(STRIP_LEN, dtype=jnp.int32)
    turn_count = positions * shift_cells.astype(jnp.int32) % STRIP_LEN
    angles = 2.0 * math.pi / STRIP_LEN * turn_count.astype(jnp.float32)
    factor_real = (window * jnp.cos(angles)).reshape(SUBGRIDS, SUB_ROWS, 1)
    factor_imag = (-window * jnp.sin(angles)).reshape(SUBGRIDS, SUB_ROWS, 1)
    return (factor_real, factor_imag)

def forward(screened, window, shift_cells):
    grid_view = screened.reshape(2, STRIP_COLS, SUB_ROWS, SUBGRIDS).astype(jnp.float32)
    section_one = jnp.einsum('tka,pcab->tpckb', fourier_table(SUB_ROWS).astype(jnp.float32), grid_view)
    real_part = section_one[0, 0] - section_one[1, 1]
    imag_part = section_one[0, 1] + section_one[1, 0]
    twist_real, twist_imag = twiddle()
    mixed = jnp.stack([real_part * twist_real - imag_part * twist_imag, real_part * twist_imag + imag_part * twist_real]).astype(jnp.bfloat16)
    section_two = jnp.einsum('tjb,pckb->tpjkc', fourier_table(SUBGRIDS).astype(jnp.float32), mixed.astype(jnp.float32))
    spec_real = section_two[0, 0] - section_two[1, 1]
    spec_imag = section_two[0, 1] + section_two[1, 0]
    factor_real, factor_imag = facet_factor(window, shift_cells)
    return jnp.concatenate([spec_real * factor_real - spec_imag * factor_imag, spec_real * factor_imag + spec_imag * factor_real], axis=2).astype(jnp.bfloat16)

def backward(all_grids, window, shift_cells, screen_phase):
    values = all_grids.astype(jnp.float32)
    grid_real = values[:, :, :STRIP_COLS]
    grid_imag = values[:, :, STRIP_COLS:]
    factor_real, factor_imag = facet_factor(window, shift_cells)
    spectral = jnp.stack([grid_real * factor_real + grid_imag * factor_imag, grid_imag * factor_real - grid_real * factor_imag]).astype(jnp.bfloat16)
    section_two = jnp.einsum('tjb,pjkc->tpckb', fourier_table(SUBGRIDS).astype(jnp.float32), spectral.astype(jnp.float32))
    half_real = section_two[0, 0] + section_two[1, 1]
    half_imag = section_two[0, 1] - section_two[1, 0]
    twist_real, twist_imag = twiddle()
    mixed = jnp.stack([half_real * twist_real + half_imag * twist_imag, half_imag * twist_real - half_real * twist_imag]).astype(jnp.bfloat16)
    section_one = jnp.einsum('tka,pckb->tpcab', fourier_table(SUB_ROWS).astype(jnp.float32), mixed.astype(jnp.float32))
    image_real = (section_one[0, 0] + section_one[1, 1]).reshape(STRIP_COLS, STRIP_LEN)
    image_imag = (section_one[0, 1] - section_one[1, 0]).reshape(STRIP_COLS, STRIP_LEN)
    phases = screen_phase.astype(jnp.float32)
    cosine = jnp.cos(phases)
    sine_part = jnp.sin(phases)
    return back_gain * jnp.stack([image_real * cosine + image_imag * sine_part, image_imag * cosine - image_real * sine_part])

def spread(cell_index, length, kernel_taps):
    tap_count = kernel_taps.shape[0]
    offset = (jnp.arange(length, dtype=jnp.int32)[None, :] - cell_index[:, None]) % length
    wanted = (jnp.arange(tap_count, dtype=jnp.int32) - tap_count // 2) % length
    matches = (offset[:, :, None] == wanted[None, None, :]).astype(jnp.float32)
    return lax.optimization_barrier(jnp.sum(matches * kernel_taps, axis=2))

def degrid(subgrid, row_cells, column_cells, plane, observed_vis, angle_table, kernel_taps):
    row_weights = spread(row_cells, SUB_ROWS, kernel_taps)
    column_weights = spread(column_cells, STRIP_COLS, kernel_taps)
    kernel_rows = jnp.dot(row_weights, subgrid, precision=lax.Precision.HIGHEST)
    model_real = lax.optimization_barrier(jnp.sum(kernel_rows[:, :STRIP_COLS] * column_weights, axis=1))
    model_imag = lax.optimization_barrier(jnp.sum(kernel_rows[:, STRIP_COLS:] * column_weights, axis=1))
    plane_pick = (plane[:, None] == jnp.arange(PLANES, dtype=jnp.int32)[None, :]).astype(jnp.float32)
    phase_angle = lax.optimization_barrier(jnp.sum(plane_pick * angle_table[None, :], axis=1))
    cosine = jnp.cos(phase_angle)
    sine_part = jnp.sin(phase_angle)
    residual_real = observed_vis[0] - (model_real * cosine - model_imag * sine_part)
    residual_imag = observed_vis[1] - (model_real * sine_part + model_imag * cosine)
    weighted = jnp.stack([residual_real * cosine + residual_imag * sine_part, residual_imag * cosine - residual_real * sine_part])
    spread_cols = jnp.concatenate([weighted[0][:, None] * column_weights, weighted[1][:, None] * column_weights], axis=1)
    adjoint = jnp.dot(row_weights.T, spread_cols, precision=lax.Precision.HIGHEST)
    return (jnp.stack([residual_real, residual_imag]), adjoint.astype(jnp.bfloat16))

def reference(model_strip, screen_angle, facet_window, facet_shift, kernel_taps, plane_angle, u_cell, v_cell, w_plane, observed):

    def screen_strip(layer_index, facet_index):
        strip_values = model_strip[facet_index].astype(jnp.float32)
        phases = screen_angle[layer_index, facet_index].astype(jnp.float32)
        cosine = jnp.cos(phases)
        sine_part = jnp.sin(phases)
        return jnp.stack([strip_values[0] * cosine - strip_values[1] * sine_part, strip_values[0] * sine_part + strip_values[1] * cosine]).astype(jnp.bfloat16)

    def layer_grids(layer_index):

        def add_facet(running, facet_index):
            screened = screen_strip(layer_index, facet_index)
            contrib = forward(screened, facet_window[facet_index], facet_shift[facet_index])
            return (running + contrib.astype(jnp.float32), None)
        start = jnp.zeros((SUBGRIDS, SUB_ROWS, 2 * STRIP_COLS), jnp.float32)
        running, _ = lax.scan(add_facet, start, jnp.arange(FACETS, dtype=jnp.int32))
        return running
    grids = lax.map(layer_grids, jnp.arange(LAYERS, dtype=jnp.int32))
    angle_rows = jnp.repeat(plane_angle, SUBGRIDS, axis=0)

    def one_subgrid(inputs):
        subgrid, row_cells, column_cells, plane, observed_vis, angle_table = inputs
        return degrid(subgrid, row_cells, column_cells, plane, observed_vis, angle_table, kernel_taps)
    residual, adjoint = lax.map(one_subgrid, (grids.reshape(LAYERS * SUBGRIDS, SUB_ROWS, 2 * STRIP_COLS), u_cell.reshape(LAYERS * SUBGRIDS, VIS), v_cell.reshape(LAYERS * SUBGRIDS, VIS), w_plane.reshape(LAYERS * SUBGRIDS, VIS), observed.reshape(LAYERS * SUBGRIDS, 2, VIS), angle_rows))
    residual = residual.reshape(LAYERS, SUBGRIDS, 2, VIS)
    adjoint = adjoint.reshape(LAYERS, SUBGRIDS, SUB_ROWS, 2 * STRIP_COLS)

    def facet_gradient(facet_index):

        def add_layer(running, layer_index):
            term = backward(adjoint[layer_index], facet_window[facet_index], facet_shift[facet_index], screen_angle[layer_index, facet_index])
            rounded = lax.optimization_barrier(term.astype(jnp.bfloat16))
            return (running + rounded.astype(jnp.float32), None)
        start = jnp.zeros((2, STRIP_COLS, STRIP_LEN), jnp.float32)
        running, _ = lax.scan(add_layer, start, jnp.arange(LAYERS, dtype=jnp.int32))
        return running
    gradient = lax.map(facet_gradient, jnp.arange(FACETS, dtype=jnp.int32))
    return (residual, gradient)
```

```python
import math

import jax
import jax.numpy as jnp
import numpy as np
from jax import lax
from jax.sharding import PartitionSpec as P

STRIP_LEN = 8192
SUB_ROWS = 64
STRIP_COLS = 64
PLANES = 8
SUBGRIDS = 128
LAYERS = 4
COLS = STRIP_COLS // LAYERS

back_gain = 8.0

Y, Z, X, CORE = 8, 2, 4, 2
FACET_INDEX = np.arange(SUBGRIDS).reshape(Y, Z, X, CORE)
STAGE_ORDER = FACET_INDEX.transpose(3, 1, 2, 0).reshape(-1)
CORE_GROUPS = FACET_INDEX.reshape(-1, CORE).tolist()
PLANE_GROUPS = FACET_INDEX.transpose(0, 3, 1, 2).reshape(-1, Z * X).tolist()
GLOBAL_INDEX = np.arange(LAYERS * SUBGRIDS).reshape(LAYERS, Y, Z, X, CORE)
LINE_GROUPS = GLOBAL_INDEX.transpose(2, 3, 4, 1, 0).reshape(-1, Y * LAYERS).tolist()


def fourier_table(length):
    positions = jnp.arange(length, dtype=jnp.int32)
    turn_count = positions[:, None] * positions[None, :] % length
    angles = 2.0 * math.pi / length * turn_count.astype(jnp.float32)
    norm_scale = 1.0 / math.sqrt(length)
    return (jnp.stack([jnp.cos(angles), -jnp.sin(angles)]) * norm_scale).astype(jnp.bfloat16)


def staged_table():
    order = jnp.asarray(STAGE_ORDER, jnp.int32)
    positions = jnp.arange(SUBGRIDS, dtype=jnp.int32)
    turn_count = order[:, None] * positions[None, :] % SUBGRIDS
    angles = 2.0 * math.pi / SUBGRIDS * turn_count.astype(jnp.float32)
    norm_scale = 1.0 / math.sqrt(SUBGRIDS)
    return (jnp.stack([jnp.cos(angles), -jnp.sin(angles)]) * norm_scale).astype(jnp.bfloat16)


def twiddle():
    low_index = jnp.arange(SUB_ROWS, dtype=jnp.int32)
    high_index = jnp.arange(SUBGRIDS, dtype=jnp.int32)
    turn_count = low_index[:, None] * high_index[None, :] % STRIP_LEN
    angles = 2.0 * math.pi / STRIP_LEN * turn_count.astype(jnp.float32)
    return (jnp.cos(angles), -jnp.sin(angles))


def facet_factor(window, shift_cells):
    positions = jnp.arange(STRIP_LEN, dtype=jnp.int32)
    turn_count = positions * shift_cells % STRIP_LEN
    angles = 2.0 * math.pi / STRIP_LEN * turn_count.astype(jnp.float32)

    def staged(values):
        return values.reshape(Y, Z, X, CORE, SUB_ROWS).transpose(3, 1, 2, 0, 4).reshape(SUBGRIDS, SUB_ROWS, 1)

    return (staged(window * jnp.cos(angles)), staged(-window * jnp.sin(angles)))


def forward(screened, factor_real, factor_imag):
    grid_view = screened.reshape(2, STRIP_COLS, SUB_ROWS, SUBGRIDS)
    section_one = jnp.einsum(
        "tka,pcab->tpckb", fourier_table(SUB_ROWS), grid_view, preferred_element_type=jnp.float32
    )
    real_part = section_one[0, 0] - section_one[1, 1]
    imag_part = section_one[0, 1] + section_one[1, 0]
    twist_real, twist_imag = twiddle()
    mixed = jnp.stack(
        [
            real_part * twist_real - imag_part * twist_imag,
            real_part * twist_imag + imag_part * twist_real,
        ]
    ).astype(jnp.bfloat16)
    section_two = jnp.einsum(
        "tjb,pckb->tpjkc", staged_table(), mixed, preferred_element_type=jnp.float32
    )
    spec_real = section_two[0, 0] - section_two[1, 1]
    spec_imag = section_two[0, 1] + section_two[1, 0]
    return jnp.concatenate(
        [
            spec_real * factor_real - spec_imag * factor_imag,
            spec_real * factor_imag + spec_imag * factor_real,
        ],
        axis=2,
    ).astype(jnp.bfloat16)


def backward(grid_real, grid_imag, factor_real, factor_imag):
    spectral = jnp.stack(
        [
            grid_real * factor_real + grid_imag * factor_imag,
            grid_imag * factor_real - grid_real * factor_imag,
        ]
    ).astype(jnp.bfloat16)
    section_two = jnp.einsum(
        "tjb,pjkc->tpckb", staged_table(), spectral, preferred_element_type=jnp.float32
    )
    half_real = section_two[0, 0] + section_two[1, 1]
    half_imag = section_two[0, 1] - section_two[1, 0]
    twist_real, twist_imag = twiddle()
    mixed = jnp.stack(
        [
            half_real * twist_real + half_imag * twist_imag,
            half_imag * twist_real - half_real * twist_imag,
        ]
    ).astype(jnp.bfloat16)
    section_one = jnp.einsum(
        "tka,pckb->tpcab", fourier_table(SUB_ROWS), mixed, preferred_element_type=jnp.float32
    )
    image_real = section_one[0, 0] + section_one[1, 1]
    image_imag = section_one[0, 1] - section_one[1, 0]
    return (image_real, image_imag)


def spread(cell_index, length, kernel_taps):
    tap_count = kernel_taps.shape[0]
    offset = (jnp.arange(length, dtype=jnp.int32)[None, :] - cell_index[:, None]) % length
    wanted = (jnp.arange(tap_count, dtype=jnp.int32) - tap_count // 2) % length
    matches = (offset[:, :, None] == wanted[None, None, :]).astype(jnp.float32)
    return jnp.sum(matches * kernel_taps, axis=2)


def degrid(subgrid, row_cells, column_cells, plane, observed_vis, angle_table, kernel_taps):
    row_weights = spread(row_cells, SUB_ROWS, kernel_taps)
    column_weights = spread(column_cells, STRIP_COLS, kernel_taps)
    kernel_rows = jnp.dot(row_weights, subgrid, precision=lax.Precision.HIGHEST)
    model_real = jnp.sum(kernel_rows[:, :STRIP_COLS] * column_weights, axis=1)
    model_imag = jnp.sum(kernel_rows[:, STRIP_COLS:] * column_weights, axis=1)
    plane_pick = (plane[:, None] == jnp.arange(PLANES, dtype=jnp.int32)[None, :]).astype(
        jnp.float32
    )
    phase_angle = jnp.sum(plane_pick * angle_table[None, :], axis=1)
    cosine = jnp.cos(phase_angle)
    sine_part = jnp.sin(phase_angle)
    residual_real = observed_vis[0] - (model_real * cosine - model_imag * sine_part)
    residual_imag = observed_vis[1] - (model_real * sine_part + model_imag * cosine)
    weighted_real = residual_real * cosine + residual_imag * sine_part
    weighted_imag = residual_imag * cosine - residual_real * sine_part
    spread_cols = jnp.concatenate(
        [weighted_real[:, None] * column_weights, weighted_imag[:, None] * column_weights], axis=1
    )
    adjoint = jnp.dot(row_weights.T, spread_cols, precision=lax.Precision.HIGHEST)
    return (jnp.stack([residual_real, residual_imag]), adjoint)


def exchange(blocks, axes, groups=None):
    return lax.all_to_all(
        blocks, axes, split_axis=0, concat_axis=0, tiled=True, axis_index_groups=groups
    )


def summed(pieces):
    return jnp.sum(pieces.astype(jnp.float32), axis=0)


def local(
    model_strip,
    screen_angle,
    facet_window,
    facet_shift,
    kernel_taps,
    plane_angle,
    u_cell,
    v_cell,
    w_plane,
    observed,
):
    quarter = STRIP_LEN // LAYERS
    strip_pieces = model_strip[0].reshape(2, LAYERS, COLS, quarter).transpose(1, 0, 2, 3)
    strip_data = exchange(strip_pieces, "layer").transpose(1, 2, 0, 3).reshape(2, COLS, STRIP_LEN)
    phases = exchange(screen_angle[0, 0].reshape(LAYERS, COLS, STRIP_LEN), "layer").astype(jnp.float32)
    cosine = jnp.cos(phases)
    sine_part = jnp.sin(phases)
    strip_values = strip_data.astype(jnp.float32)
    screened = jnp.stack(
        [
            strip_values[0] * cosine - strip_values[1] * sine_part,
            strip_values[0] * sine_part + strip_values[1] * cosine,
        ]
    ).astype(jnp.bfloat16)
    factor_real, factor_imag = facet_factor(facet_window[0], facet_shift[0])
    contrib = forward(screened.reshape(2, STRIP_COLS, STRIP_LEN), factor_real, factor_imag)

    row_cols = (SUB_ROWS, 2 * STRIP_COLS)
    pair_sum = summed(exchange(contrib.reshape(CORE, SUBGRIDS // CORE, *row_cols), "facet", CORE_GROUPS))
    plane_sum = summed(
        exchange(pair_sum.astype(jnp.bfloat16).reshape(Z * X, Y, *row_cols), "facet", PLANE_GROUPS)
    )
    packed = (
        plane_sum.astype(jnp.bfloat16)
        .reshape(Y, 4, SUB_ROWS // 4, 2, LAYERS, COLS)
        .transpose(0, 4, 2, 1, 3, 5)
        .reshape(Y * LAYERS, SUB_ROWS // 4, 2 * STRIP_COLS)
    )
    line_sum = summed(
        exchange(packed, ("layer", "facet"), LINE_GROUPS).reshape(
            Y, LAYERS, SUB_ROWS // 4, 2 * STRIP_COLS
        )
    )
    subgrid = (
        line_sum.reshape(LAYERS, SUB_ROWS // 4, 4, 2, COLS)
        .transpose(2, 1, 3, 0, 4)
        .reshape(SUB_ROWS, 2 * STRIP_COLS)
    )

    residual, adjoint = degrid(
        subgrid, u_cell[0, 0], v_cell[0, 0], w_plane[0, 0], observed[0, 0], plane_angle[0], kernel_taps
    )

    sent = (
        adjoint.astype(jnp.bfloat16)
        .reshape(4, SUB_ROWS // 4, 2, LAYERS, COLS)
        .transpose(3, 1, 0, 2, 4)
        .reshape(1, LAYERS, SUB_ROWS // 4, 2 * STRIP_COLS)
    )
    piece = (SUB_ROWS // 4, 2 * STRIP_COLS)
    line = exchange(
        jnp.broadcast_to(sent, (Y, LAYERS, *piece)).reshape(Y * LAYERS, *piece),
        ("layer", "facet"),
        LINE_GROUPS,
    )
    line = (
        line.reshape(Y, LAYERS, SUB_ROWS // 4, 4, 2, COLS)
        .transpose(0, 3, 2, 4, 1, 5)
        .reshape(Y, *row_cols)
    )
    plane = exchange(jnp.broadcast_to(line[None], (Z * X, Y, *row_cols)), "facet", PLANE_GROUPS)
    grids = exchange(
        jnp.broadcast_to(plane[None], (CORE, Z * X, Y, *row_cols)), "facet", CORE_GROUPS
    ).reshape(SUBGRIDS, *row_cols)
    grids = grids.astype(jnp.float32)
    image_real, image_imag = backward(
        grids[:, :, :STRIP_COLS], grids[:, :, STRIP_COLS:], factor_real, factor_imag)
    image_real = image_real.reshape(LAYERS, COLS, STRIP_LEN)
    image_imag = image_imag.reshape(LAYERS, COLS, STRIP_LEN)
    total = back_gain * jnp.stack(
        [
            jnp.sum(image_real * cosine + image_imag * sine_part, axis=0),
            jnp.sum(image_imag * cosine - image_real * sine_part, axis=0),
        ]
    )
    leaving = total.astype(jnp.bfloat16).reshape(2, COLS, LAYERS, quarter).transpose(2, 0, 1, 3)
    gradient = (
        exchange(leaving, "layer")
        .transpose(1, 0, 2, 3)
        .reshape(1, 2, STRIP_COLS, quarter)
        .astype(jnp.float32)
    )
    return (residual[None, None], gradient)


def solution(mesh):
    return jax.shard_map(
        local,
        mesh=mesh,
        in_specs=(
            P("facet", None, None, "layer"),
            P("layer", "facet", None, None),
            P("facet", None),
            P("facet"),
            P(),
            P("layer", None),
            P("layer", "facet", None),
            P("layer", "facet", None),
            P("layer", "facet", None),
            P("layer", "facet", None, None),
        ),
        out_specs=(P("layer", "facet", None, None), P("facet", None, None, "layer")),
        check_vma=False,
    )
```

```python
import math

import jax
import jax.numpy as jnp
import numpy as np
from jax import lax
from jax.experimental import pallas as pl
from jax.experimental.pallas import tpu as pltpu
from jax.sharding import PartitionSpec as P

STRIP_LEN = 8192
SUB_ROWS = 64
STRIP_COLS = 64
PLANES = 8
SUBGRIDS = 128
LAYERS = 4
COLS = STRIP_COLS // LAYERS
QUARTER = STRIP_LEN // LAYERS
LANES = 128
BLOCKS = QUARTER // LANES

back_gain = 8.0

Y, Z, X, CORE = 8, 2, 4, 2
ZX = Z * X
FACET_INDEX = np.arange(SUBGRIDS).reshape(Y, Z, X, CORE)
STAGE_ORDER = FACET_INDEX.transpose(3, 1, 2, 0).reshape(-1)
PLANE_GROUPS = FACET_INDEX.transpose(0, 3, 1, 2).reshape(-1, ZX).tolist()
GLOBAL_INDEX = np.arange(LAYERS * SUBGRIDS).reshape(LAYERS, Y, Z, X, CORE)
LINE_GROUPS = GLOBAL_INDEX.transpose(2, 3, 4, 1, 0).reshape(-1, Y * LAYERS).tolist()
CORE_SWAP = [(i, i ^ 1) for i in range(SUBGRIDS)]

VMEM_LIMIT = 48 * 1024 * 1024


def even_series(function, degree):
    series = np.polynomial.chebyshev.Chebyshev.interpolate(
        lambda t: function(np.sqrt(np.maximum((t + 1.0) * 0.5, 0.0)) * math.pi), degree
    )
    return [float(value) for value in np.polynomial.chebyshev.cheb2poly(series.coef)]


COSINE_SERIES = even_series(np.cos, 8)
SINE_SERIES = even_series(lambda x: np.sinc(x / math.pi), 8)


def phase_parts(angle):
    t = angle * angle * (2.0 / (math.pi * math.pi)) - 1.0
    cosine = jnp.full_like(t, COSINE_SERIES[-1])
    sine = jnp.full_like(t, SINE_SERIES[-1])
    for value in COSINE_SERIES[-2::-1]:
        cosine = cosine * t + value
    for value in SINE_SERIES[-2::-1]:
        sine = sine * t + value
    return cosine, sine * angle


def fourier_table(rows, length):
    turn_count = rows[:, None] * np.arange(length)[None, :] % length
    angles = 2.0 * math.pi / length * turn_count
    table = np.stack([np.cos(angles), -np.sin(angles)]) / math.sqrt(length)
    return table.astype(np.float32).astype(jnp.bfloat16)


def twiddle():
    turn_count = np.arange(SUB_ROWS)[:, None] * np.arange(LANES)[None, :] % STRIP_LEN
    angles = 2.0 * math.pi / STRIP_LEN * turn_count
    return (np.cos(angles).astype(np.float32), (-np.sin(angles)).astype(np.float32))


def first_tables():
    real, imag = fourier_table(np.arange(SUB_ROWS), SUB_ROWS)
    ahead = np.block([[real, -imag], [imag, real]])
    back = np.block([[real.T, imag.T], [-imag.T, real.T]])
    return (ahead, back)


def second_tables(order):
    real, imag = fourier_table(order, SUBGRIDS)
    ahead = np.block([[real.T, imag.T], [-imag.T, real.T]])
    back = np.block([[real, -imag], [imag, real]])
    return (ahead, back)


def pack_table():
    table = np.zeros((4, 2, LAYERS, COLS, LAYERS, 4, 2, COLS), np.float32)
    for r in range(4):
        for p in range(2):
            for layer in range(LAYERS):
                for c in range(COLS):
                    table[r, p, layer, c, layer, r, p, c] = 1.0
    return table.reshape(4 * LANES, 4 * LANES).astype(jnp.bfloat16)


def facet_factor(window, shift_cells, swapped):
    def staged(values):
        ordered = values.reshape(Y, Z, X, CORE, SUB_ROWS).transpose(4, 3, 1, 2, 0)
        mine = ordered.reshape(SUB_ROWS, CORE, SUBGRIDS // CORE)
        return jnp.where(swapped, mine[:, ::-1], mine).reshape(SUB_ROWS, SUBGRIDS)

    positions = jnp.arange(STRIP_LEN, dtype=jnp.int32)
    turn_count = positions * shift_cells % STRIP_LEN
    angles = 2.0 * math.pi / STRIP_LEN * turn_count.astype(jnp.float32)
    return (staged(window * jnp.cos(angles)), staged(-window * jnp.sin(angles)))


def forward_kernel(
    layer_ref, p0, p1, p2, p3, twist_real, twist_imag, first, second, factor_real, factor_imag,
    mine_ref, other_ref, screened, half,
):
    pieces = (p0, p1, p2, p3)
    q = layer_ref[0]
    table = first[...]
    for j in range(LAYERS):
        layer = (q + LAYERS - j) & 3

        def screen_block(t, carry, j=j):
            lanes = pl.ds(pl.multiple_of(t * LANES, LANES), LANES)
            for i in range(LAYERS):
                nq = (q + LAYERS - i) & 3
                cosine, sine = phase_parts(pieces[j][2 + nq, :, lanes].astype(jnp.float32))
                real = pieces[i][0, :, lanes].astype(jnp.float32)
                imag = pieces[i][1, :, lanes].astype(jnp.float32)
                rows = pl.ds(pl.multiple_of((nq * BLOCKS + t) * COLS, COLS), COLS)
                screened[0, rows, :] = real * cosine - imag * sine
                screened[1, rows, :] = real * sine + imag * cosine
            return carry

        lax.fori_loop(0, BLOCKS, screen_block, 0)

        def first_block(pair, carry, layer=layer):
            def column(part, c):
                return screened[part, pl.ds(c, SUB_ROWS, stride=COLS), :]

            c = pair * 2
            data = jnp.concatenate(
                [
                    jnp.concatenate([column(0, c), column(1, c)], axis=0),
                    jnp.concatenate([column(0, c + 1), column(1, c + 1)], axis=0),
                ],
                axis=1,
            ).astype(jnp.bfloat16)
            mixed = jnp.dot(table, data, preferred_element_type=jnp.float32)
            for h in range(2):
                real = mixed[:SUB_ROWS, h * LANES : (h + 1) * LANES]
                imag = mixed[SUB_ROWS:, h * LANES : (h + 1) * LANES]
                rows = pl.ds(layer * COLS + c + h, SUB_ROWS, stride=STRIP_COLS)
                half[0, rows, :] = real * twist_real[...] - imag * twist_imag[...]
                half[1, rows, :] = real * twist_imag[...] + imag * twist_real[...]
            return carry

        lax.fori_loop(0, COLS // 2, first_block, 0)

    weights = second[...]

    def second_block(pair, carry):
        rows = pl.ds(pl.multiple_of(pair * 2 * STRIP_COLS, 2 * STRIP_COLS), 2 * STRIP_COLS)
        data = jnp.concatenate([half[0, rows, :], half[1, rows, :]], axis=1).astype(jnp.bfloat16)
        spectrum = jnp.dot(data, weights, preferred_element_type=jnp.float32)
        blocks = []
        for h in range(2):
            real = spectrum[h * STRIP_COLS : (h + 1) * STRIP_COLS, :LANES]
            imag = spectrum[h * STRIP_COLS : (h + 1) * STRIP_COLS, LANES:]
            fr = factor_real[pl.ds(pair * 2 + h, 1), :]
            fi = factor_imag[pl.ds(pair * 2 + h, 1), :]
            turned = jnp.concatenate([real * fr - imag * fi, real * fi + imag * fr], axis=0).T
            blocks.append(turned.reshape(CORE * ZX, Y, LANES))
        both = jnp.concatenate(blocks, axis=1).astype(jnp.bfloat16)
        place = pl.ds(pl.multiple_of(pair * 2 * Y, 2 * Y), 2 * Y)
        mine_ref[:, place, :] = both[:ZX]
        other_ref[:, place, :] = both[ZX:]
        return carry

    lax.fori_loop(0, SUB_ROWS // 2, second_block, 0, unroll=2)


def pack_kernel(pieces, table, out_ref, total):
    total[...] = jnp.sum(pieces[...].astype(jnp.float32), axis=0)
    rows = []
    for y in range(Y):
        block = total[pl.ds(y, SUB_ROWS, stride=Y), :]
        rows.append(jnp.concatenate([block[r * 16 : (r + 1) * 16] for r in range(4)], axis=1))
    data = jnp.concatenate(rows, axis=0).astype(jnp.bfloat16)
    packed = jnp.dot(data, table[...], preferred_element_type=jnp.float32).astype(jnp.bfloat16)
    for y in range(Y):
        for layer in range(LAYERS):
            out_ref[y * LAYERS + layer] = packed[
                y * 16 : (y + 1) * 16, layer * LANES : (layer + 1) * LANES
            ]


def unpack_kernel(line, table, out_ref, total):
    data = jnp.concatenate(
        [
            jnp.concatenate([line[y * LAYERS + layer] for layer in range(LAYERS)], axis=1)
            for y in range(Y)
        ],
        axis=0,
    )
    grids = lax.dot_general(
        data, table[...], (((1,), (1,)), ((), ())), preferred_element_type=jnp.float32
    )
    for y in range(Y):
        for r in range(4):
            total[pl.ds(r * 16 * Y + y, 16, stride=Y), :] = grids[
                y * 16 : (y + 1) * 16, r * LANES : (r + 1) * LANES
            ]
    block = total[...].astype(jnp.bfloat16)
    for copy in range(ZX):
        out_ref[copy] = block


def backward_kernel(
    layer_ref, mine, other, p0, p1, p2, p3, twist_real, twist_imag, first, second, factor_real,
    factor_imag, o0, o1, o2, o3, half, phases, total,
):
    pieces = (p0, p1, p2, p3)
    q = layer_ref[0]
    rows_of = SUB_ROWS * COLS
    for j in range(LAYERS):

        def phase_block(t, carry, j=j):
            lanes = pl.ds(pl.multiple_of(t * LANES, LANES), LANES)
            for nq in range(LAYERS):
                cosine, sine = phase_parts(pieces[j][2 + nq, :, lanes].astype(jnp.float32))
                rows = pl.ds(
                    pl.multiple_of(j * rows_of + (nq * BLOCKS + t) * COLS, COLS), COLS
                )
                phases[0, rows, :] = cosine
                phases[1, rows, :] = sine
            return carry

        lax.fori_loop(0, BLOCKS, phase_block, 0)

    weights = second[...]

    def second_block(pair, carry):
        place = pl.ds(pl.multiple_of(pair * 2 * Y, 2 * Y), 2 * Y)
        both = jnp.concatenate([mine[:, place, :], other[:, place, :]], axis=0).astype(jnp.float32)
        data = []
        for h in range(2):
            turned = both[:, h * Y : (h + 1) * Y, :].reshape(SUBGRIDS, LANES).T
            real = turned[:STRIP_COLS]
            imag = turned[STRIP_COLS:]
            fr = factor_real[pl.ds(pair * 2 + h, 1), :]
            fi = factor_imag[pl.ds(pair * 2 + h, 1), :]
            data.append(
                jnp.concatenate([real * fr + imag * fi, imag * fr - real * fi], axis=1)
            )
        data = jnp.concatenate(data, axis=0).astype(jnp.bfloat16)
        mixed = jnp.dot(data, weights, preferred_element_type=jnp.float32)
        for h in range(2):
            real = mixed[h * STRIP_COLS : (h + 1) * STRIP_COLS, :LANES]
            imag = mixed[h * STRIP_COLS : (h + 1) * STRIP_COLS, LANES:]
            tr = twist_real[pl.ds(pair * 2 + h, 1), :]
            ti = twist_imag[pl.ds(pair * 2 + h, 1), :]
            rows = pl.ds(pair * 2 + h, STRIP_COLS, stride=SUB_ROWS)
            half[0, rows, :] = real * tr + imag * ti
            half[1, rows, :] = imag * tr - real * ti
        return carry

    lax.fori_loop(0, SUB_ROWS // 2, second_block, 0, unroll=2)

    table = first[...]

    def first_block(pair, carry):
        c = pair * 2
        sums = [None] * 4
        for j in range(LAYERS):
            layer = (q + LAYERS - j) & 3

            def column(part, h):
                start = (layer * COLS + c + h) * SUB_ROWS
                return half[part, pl.ds(pl.multiple_of(start, SUB_ROWS), SUB_ROWS), :]

            data = jnp.concatenate(
                [
                    jnp.concatenate([column(0, 0), column(1, 0)], axis=0),
                    jnp.concatenate([column(0, 1), column(1, 1)], axis=0),
                ],
                axis=1,
            ).astype(jnp.bfloat16)
            image = jnp.dot(table, data, preferred_element_type=jnp.float32)
            for h in range(2):
                real = image[:SUB_ROWS, h * LANES : (h + 1) * LANES]
                imag = image[SUB_ROWS:, h * LANES : (h + 1) * LANES]
                rows = pl.ds(j * rows_of + c + h, SUB_ROWS, stride=COLS)
                cosine = phases[0, rows, :]
                sine = phases[1, rows, :]
                for part, term in enumerate(
                    (real * cosine + imag * sine, imag * cosine - real * sine)
                ):
                    place = 2 * h + part
                    sums[place] = term if j == 0 else sums[place] + term
        for h in range(2):
            for part in range(2):
                total[part, pl.ds(c + h, SUB_ROWS, stride=COLS), :] = back_gain * sums[2 * h + part]
        return carry

    lax.fori_loop(0, COLS // 2, first_block, 0)

    def leave_block(t, carry):
        lanes = pl.ds(pl.multiple_of(t * LANES, LANES), LANES)
        for i, out_ref in enumerate((o0, o1, o2, o3)):
            nq = (q + i) & 3
            rows = pl.ds(pl.multiple_of((nq * BLOCKS + t) * COLS, COLS), COLS)
            for part in range(2):
                out_ref[part, :, lanes] = total[part, rows, :].astype(out_ref.dtype)
        return carry

    lax.fori_loop(0, BLOCKS, leave_block, 0)


def join_kernel(layer_ref, r0, r1, r2, r3, out_ref):
    q = layer_ref[0]
    for i, piece in enumerate((r0, r1, r2, r3)):
        source = (q + LAYERS - i) & 3
        rows = pl.ds(pl.multiple_of(source * COLS, COLS), COLS)
        for part in range(2):
            out_ref[part, rows, :] = piece[part].astype(jnp.float32)


def on_core(kernel, name, out_shape, scratch=(), scalars=0, inputs=1):
    specs = [pl.BlockSpec(memory_space=pltpu.SMEM)] * scalars
    specs += [pl.BlockSpec(memory_space=pltpu.VMEM)] * inputs
    is_list = isinstance(out_shape, (list, tuple))
    one = pl.BlockSpec(memory_space=pltpu.VMEM)
    return pl.pallas_call(
        kernel,
        name=name,
        out_shape=out_shape,
        in_specs=specs,
        out_specs=[one] * len(out_shape) if is_list else one,
        scratch_shapes=list(scratch),
        compiler_params=pltpu.CompilerParams(vmem_limit_bytes=VMEM_LIMIT),
    )


def shaped(shape, kind):
    return jax.ShapeDtypeStruct(shape, kind)


def forward(layer, pieces, factor_real, factor_imag, second):
    blocks = shaped((ZX, SUB_ROWS * Y, LANES), jnp.bfloat16)
    twist_real, twist_imag = twiddle()
    return on_core(
        forward_kernel,
        "ahead",
        [blocks, blocks],
        (
            pltpu.VMEM((2, SUB_ROWS * COLS, LANES), jnp.float32),
            pltpu.VMEM((2, SUB_ROWS * STRIP_COLS, LANES), jnp.float32),
        ),
        1,
        10,
    )(layer, *pieces, twist_real, twist_imag, first_tables()[0], second, factor_real, factor_imag)


def backward(layer, mine, other, pieces, factor_real, factor_imag, second):
    twist_real, twist_imag = twiddle()
    piece = (2, COLS, QUARTER)
    return on_core(
        backward_kernel,
        "back",
        [shaped(piece, jnp.float32)] + [shaped(piece, jnp.bfloat16)] * 3,
        (
            pltpu.VMEM((2, SUB_ROWS * STRIP_COLS, LANES), jnp.float32),
            pltpu.VMEM((2, LAYERS * SUB_ROWS * COLS, LANES), jnp.float32),
            pltpu.VMEM((2, SUB_ROWS * COLS, LANES), jnp.float32),
        ),
        1,
        12,
    )(
        layer, mine, other, *pieces, twist_real, twist_imag, first_tables()[1], second,
        factor_real, factor_imag,
    )


def spread(cell_index, length, kernel_taps):
    tap_count = kernel_taps.shape[0]
    offset = (jnp.arange(length, dtype=jnp.int32)[None, :] - cell_index[:, None]) % length
    wanted = (jnp.arange(tap_count, dtype=jnp.int32) - tap_count // 2) % length
    matches = (offset[:, :, None] == wanted[None, None, :]).astype(jnp.float32)
    return jnp.sum(matches * kernel_taps, axis=2)


def degrid(subgrid, row_cells, column_cells, plane, observed_vis, angle_table, kernel_taps):
    row_weights = spread(row_cells, SUB_ROWS, kernel_taps)
    column_weights = spread(column_cells, STRIP_COLS, kernel_taps)
    kernel_rows = jnp.dot(row_weights, subgrid, precision=lax.Precision.HIGHEST)
    model_real = jnp.sum(kernel_rows[:, :STRIP_COLS] * column_weights, axis=1)
    model_imag = jnp.sum(kernel_rows[:, STRIP_COLS:] * column_weights, axis=1)
    plane_pick = (plane[:, None] == jnp.arange(PLANES, dtype=jnp.int32)[None, :]).astype(
        jnp.float32
    )
    phase_angle = jnp.sum(plane_pick * angle_table[None, :], axis=1)
    cosine = jnp.cos(phase_angle)
    sine_part = jnp.sin(phase_angle)
    residual_real = observed_vis[0] - (model_real * cosine - model_imag * sine_part)
    residual_imag = observed_vis[1] - (model_real * sine_part + model_imag * cosine)
    weighted_real = residual_real * cosine + residual_imag * sine_part
    weighted_imag = residual_imag * cosine - residual_real * sine_part
    spread_cols = jnp.concatenate(
        [weighted_real[:, None] * column_weights, weighted_imag[:, None] * column_weights], axis=1
    )
    adjoint = jnp.dot(row_weights.T, spread_cols, precision=lax.Precision.HIGHEST)
    return (jnp.stack([residual_real, residual_imag]), adjoint)


def exchange(blocks, axes, groups=None):
    return lax.all_to_all(
        blocks, axes, split_axis=0, concat_axis=0, tiled=True, axis_index_groups=groups
    )


def local(
    model_strip,
    screen_angle,
    facet_window,
    facet_shift,
    kernel_taps,
    plane_angle,
    u_cell,
    v_cell,
    w_plane,
    observed,
):
    layer = lax.axis_index("layer").astype(jnp.int32)
    swapped = lax.axis_index("facet") % CORE == 1
    layer_of = layer.reshape(1)

    joined = jnp.concatenate(
        [
            model_strip[0].reshape(2, LAYERS, COLS, QUARTER).transpose(1, 0, 2, 3),
            screen_angle[0, 0].reshape(LAYERS, COLS, LAYERS, QUARTER).transpose(0, 2, 1, 3),
        ],
        axis=1,
    )
    pieces = []
    for shift in range(LAYERS):
        piece = lax.dynamic_index_in_dim(joined, (layer + shift) % LAYERS, 0, keepdims=False)
        if shift:
            piece = lax.ppermute(piece, "layer", [(i, (i + shift) % LAYERS) for i in range(LAYERS)])
        pieces.append(piece)

    factor_real, factor_imag = facet_factor(facet_window[0], facet_shift[0], swapped)
    plain = second_tables(STAGE_ORDER)
    crossed = second_tables(np.roll(STAGE_ORDER, SUBGRIDS // CORE))
    second_ahead = jnp.where(swapped, crossed[0], plain[0])
    second_back = jnp.where(swapped, crossed[1], plain[1])
    mine, other = forward(layer_of, pieces, factor_real, factor_imag, second_ahead)

    arrived = lax.ppermute(other, "facet", CORE_SWAP)
    pair_sum = (mine.astype(jnp.float32) + arrived.astype(jnp.float32)).astype(jnp.bfloat16)
    plane_terms = exchange(pair_sum, "facet", PLANE_GROUPS)
    table = pack_table()
    piece = (SUB_ROWS // 4, 2 * STRIP_COLS)
    packed = on_core(
        pack_kernel,
        "pack",
        shaped((Y * LAYERS, *piece), jnp.bfloat16),
        (pltpu.VMEM((SUB_ROWS * Y, LANES), jnp.float32),),
        0,
        2,
    )(plane_terms, table)
    line_sum = jnp.sum(
        exchange(packed, ("layer", "facet"), LINE_GROUPS)
        .reshape(Y, LAYERS, *piece)
        .astype(jnp.float32),
        axis=0,
    )
    subgrid = (
        line_sum.reshape(LAYERS, SUB_ROWS // 4, 4, 2, COLS)
        .transpose(2, 1, 3, 0, 4)
        .reshape(SUB_ROWS, 2 * STRIP_COLS)
    )

    residual, adjoint = degrid(
        subgrid, u_cell[0, 0], v_cell[0, 0], w_plane[0, 0], observed[0, 0], plane_angle[0], kernel_taps
    )

    sent = (
        adjoint.astype(jnp.bfloat16)
        .reshape(4, SUB_ROWS // 4, 2, LAYERS, COLS)
        .transpose(3, 1, 0, 2, 4)
        .reshape(1, LAYERS, *piece)
    )
    line = exchange(
        jnp.broadcast_to(sent, (Y, LAYERS, *piece)).reshape(Y * LAYERS, *piece),
        ("layer", "facet"),
        LINE_GROUPS,
    )
    copies = on_core(
        unpack_kernel,
        "unpack",
        shaped((ZX, SUB_ROWS * Y, LANES), jnp.bfloat16),
        (pltpu.VMEM((SUB_ROWS * Y, LANES), jnp.float32),),
        0,
        2,
    )(line, table)
    mine_grids = exchange(copies, "facet", PLANE_GROUPS)
    other_grids = lax.ppermute(mine_grids, "facet", CORE_SWAP)
    leaving = backward(
        layer_of, mine_grids, other_grids, pieces, factor_real, factor_imag, second_back
    )
    arriving = [leaving[0]]
    for shift in range(1, LAYERS):
        arriving.append(
            lax.ppermute(
                leaving[shift], "layer", [(i, (i + shift) % LAYERS) for i in range(LAYERS)]
            )
        )
    gradient = on_core(
        join_kernel, "join", shaped((2, STRIP_COLS, QUARTER), jnp.float32), (), 1, 4
    )(layer_of, *arriving)
    return (residual[None, None], gradient[None])


def solution(mesh):
    return jax.shard_map(
        local,
        mesh=mesh,
        in_specs=(
            P("facet", None, None, "layer"),
            P("layer", "facet", None, None),
            P("facet", None),
            P("facet"),
            P(),
            P("layer", None),
            P("layer", "facet", None),
            P("layer", "facet", None),
            P("layer", "facet", None),
            P("layer", "facet", None, None),
        ),
        out_specs=(P("layer", "facet", None, None), P("facet", None, None, "layer")),
        check_vma=False,
    )
```

```python
import math

import jax
import jax.numpy as jnp
import numpy as np
from jax import lax
from jax.experimental import pallas as pl
from jax.experimental.pallas import tpu as pltpu
from jax.sharding import PartitionSpec as P

STRIP_LEN = 8192
SUB_ROWS = 64
STRIP_COLS = 64
PLANES = 8
SUBGRIDS = 128
LAYERS = 4
COLS = STRIP_COLS // LAYERS
QUARTER = STRIP_LEN // LAYERS
LANES = 128
BLOCKS = QUARTER // LANES

back_gain = 8.0

Y, Z, X, CORE = 8, 2, 4, 2
ZX = Z * X
FACET_INDEX = np.arange(SUBGRIDS).reshape(Y, Z, X, CORE)
STAGE_ORDER = FACET_INDEX.transpose(3, 1, 2, 0).reshape(-1)
PLANE_GROUPS = FACET_INDEX.transpose(0, 3, 1, 2).reshape(-1, ZX).tolist()
GLOBAL_INDEX = np.arange(LAYERS * SUBGRIDS).reshape(LAYERS, Y, Z, X, CORE)
LINE_GROUPS = GLOBAL_INDEX.transpose(2, 3, 4, 1, 0).reshape(-1, Y * LAYERS).tolist()
CORE_SWAP = [(i, i ^ 1) for i in range(SUBGRIDS)]

VMEM_LIMIT = 32 * 1024 * 1024

COL_PITCH = 24
LINE_PITCH = 72
PHASE_ROWS = SUB_ROWS * COL_PITCH


def even_series(function, degree):
    series = np.polynomial.chebyshev.Chebyshev.interpolate(
        lambda t: function(np.sqrt(np.maximum((t + 1.0) * 0.5, 0.0)) * math.pi), degree
    )
    return [float(value) for value in np.polynomial.chebyshev.cheb2poly(series.coef)]


COSINE_SERIES = even_series(np.cos, 8)
SINE_SERIES = even_series(lambda x: np.sinc(x / math.pi), 8)


def phase_parts(angle):
    t = angle * angle * (2.0 / (math.pi * math.pi)) - 1.0
    cosine = jnp.full_like(t, COSINE_SERIES[-1])
    sine = jnp.full_like(t, SINE_SERIES[-1])
    for value in COSINE_SERIES[-2::-1]:
        cosine = cosine * t + value
    for value in SINE_SERIES[-2::-1]:
        sine = sine * t + value
    return cosine, sine * angle


def fourier_table(rows, length):
    turn_count = rows[:, None] * np.arange(length)[None, :] % length
    angles = 2.0 * math.pi / length * turn_count
    table = np.stack([np.cos(angles), -np.sin(angles)]) / math.sqrt(length)
    return table.astype(np.float32).astype(jnp.bfloat16)


def twiddle():
    turn_count = np.arange(SUB_ROWS)[:, None] * np.arange(LANES)[None, :] % STRIP_LEN
    angles = 2.0 * math.pi / STRIP_LEN * turn_count
    return (np.cos(angles).astype(np.float32), (-np.sin(angles)).astype(np.float32))


def first_tables():
    real, imag = fourier_table(np.arange(SUB_ROWS), SUB_ROWS)
    ahead = np.block([[real, -imag], [imag, real]])
    back = np.block([[real.T, imag.T], [-imag.T, real.T]])
    return (ahead, back)


def second_tables(order):
    real, imag = fourier_table(order, SUBGRIDS)
    ahead = np.block([[real.T, imag.T], [-imag.T, real.T]])
    back = np.block([[real, -imag], [imag, real]])
    return (ahead, back)


def pack_table():
    table = np.zeros((4, 2, LAYERS, COLS, LAYERS, 4, 2, COLS), np.float32)
    for r in range(4):
        for p in range(2):
            for layer in range(LAYERS):
                for c in range(COLS):
                    table[r, p, layer, c, layer, r, p, c] = 1.0
    return table.reshape(4 * LANES, 4 * LANES).astype(jnp.bfloat16)


def facet_factor(window, shift_cells, swapped):
    def staged(values):
        ordered = values.reshape(Y, Z, X, CORE, SUB_ROWS).transpose(4, 3, 1, 2, 0)
        mine = ordered.reshape(SUB_ROWS, CORE, SUBGRIDS // CORE)
        return jnp.where(swapped, mine[:, ::-1], mine).reshape(SUB_ROWS, SUBGRIDS)

    positions = jnp.arange(STRIP_LEN, dtype=jnp.int32)
    turn_count = positions * shift_cells % STRIP_LEN
    angles = 2.0 * math.pi / STRIP_LEN * turn_count.astype(jnp.float32)
    return (staged(window * jnp.cos(angles)), staged(-window * jnp.sin(angles)))


def forward_kernel(
    pieces, twist_real, twist_imag, first, second, factor_real, factor_imag,
    mine_ref, other_ref, phases, strip, half,
):
    table = first[...]

    def strip_block(t, carry):
        lanes = pl.ds(pl.multiple_of(t * LANES, LANES), LANES)
        for nq in range(LAYERS):
            rows = pl.ds(pl.multiple_of((nq * BLOCKS + t) * COL_PITCH, 8), COLS)
            for part in range(2):
                strip[part, rows, :] = pieces[nq, part, :, lanes].astype(jnp.float32)
        return carry

    lax.fori_loop(0, BLOCKS, strip_block, 0, unroll=2)
    for layer in range(LAYERS):

        def phase_block(t, carry, layer=layer):
            lanes = pl.ds(pl.multiple_of(t * LANES, LANES), LANES)
            for nq in range(LAYERS):
                cosine, sine = phase_parts(pieces[layer, 2 + nq, :, lanes].astype(jnp.float32))
                rows = pl.ds(
                    pl.multiple_of(layer * PHASE_ROWS + (nq * BLOCKS + t) * COL_PITCH, 8), COLS
                )
                phases[0, rows, :] = cosine
                phases[1, rows, :] = sine
            return carry

        lax.fori_loop(0, BLOCKS, phase_block, 0, unroll=4)

        def first_block(pair, carry, layer=layer):
            c = pair * 2
            data = []
            for h in range(2):
                column = pl.ds(c + h, SUB_ROWS, stride=COL_PITCH)
                turn = pl.ds(layer * PHASE_ROWS + c + h, SUB_ROWS, stride=COL_PITCH)
                real, imag = strip[0, column, :], strip[1, column, :]
                cosine, sine = phases[0, turn, :], phases[1, turn, :]
                data.append(
                    jnp.concatenate(
                        [real * cosine - imag * sine, real * sine + imag * cosine], axis=0
                    )
                )
            data = jnp.concatenate(data, axis=1).astype(jnp.bfloat16)
            mixed = jnp.dot(table, data, preferred_element_type=jnp.float32)
            for h in range(2):
                real = mixed[:SUB_ROWS, h * LANES : (h + 1) * LANES]
                imag = mixed[SUB_ROWS:, h * LANES : (h + 1) * LANES]
                rows = pl.ds(layer * COLS + c + h, SUB_ROWS, stride=LINE_PITCH)
                half[0, rows, :] = real * twist_real[...] - imag * twist_imag[...]
                half[1, rows, :] = real * twist_imag[...] + imag * twist_real[...]
            return carry

        lax.fori_loop(0, COLS // 2, first_block, 0, unroll=4)

    weights = second[...]

    def second_block(pair, carry):
        data = []
        for h in range(2):
            rows = pl.ds(pl.multiple_of((pair * 2 + h) * LINE_PITCH, 8), STRIP_COLS)
            data.append(jnp.concatenate([half[0, rows, :], half[1, rows, :]], axis=1))
        data = jnp.concatenate(data, axis=0).astype(jnp.bfloat16)
        spectrum = jnp.dot(data, weights, preferred_element_type=jnp.float32)
        blocks = []
        for h in range(2):
            real = spectrum[h * STRIP_COLS : (h + 1) * STRIP_COLS, :LANES]
            imag = spectrum[h * STRIP_COLS : (h + 1) * STRIP_COLS, LANES:]
            fr = factor_real[pl.ds(pair * 2 + h, 1), :]
            fi = factor_imag[pl.ds(pair * 2 + h, 1), :]
            turned = jnp.concatenate([real * fr - imag * fi, real * fi + imag * fr], axis=0).T
            blocks.append(turned.reshape(CORE * ZX, Y, LANES))
        both = jnp.concatenate(blocks, axis=1).astype(jnp.bfloat16)
        place = pl.ds(pl.multiple_of(pair * 2 * Y, 2 * Y), 2 * Y)
        mine_ref[:, place, :] = both[:ZX]
        other_ref[:, place, :] = both[ZX:]
        return carry

    lax.fori_loop(0, SUB_ROWS // 2, second_block, 0, unroll=8)


def pack_kernel(pieces, table, out_ref, total):
    total[...] = jnp.sum(pieces[...].astype(jnp.float32), axis=0)
    rows = []
    for y in range(Y):
        block = total[pl.ds(y, SUB_ROWS, stride=Y), :]
        rows.append(jnp.concatenate([block[r * 16 : (r + 1) * 16] for r in range(4)], axis=1))
    data = jnp.concatenate(rows, axis=0).astype(jnp.bfloat16)
    packed = jnp.dot(data, table[...], preferred_element_type=jnp.float32).astype(jnp.bfloat16)
    for y in range(Y):
        for layer in range(LAYERS):
            out_ref[y * LAYERS + layer] = packed[
                y * 16 : (y + 1) * 16, layer * LANES : (layer + 1) * LANES
            ]


def unpack_kernel(line, table, out_ref, total):
    data = jnp.concatenate(
        [
            jnp.concatenate([line[y * LAYERS + layer] for layer in range(LAYERS)], axis=1)
            for y in range(Y)
        ],
        axis=0,
    )
    grids = lax.dot_general(
        data, table[...], (((1,), (1,)), ((), ())), preferred_element_type=jnp.float32
    )
    for y in range(Y):
        for r in range(4):
            total[pl.ds(r * 16 * Y + y, 16, stride=Y), :] = grids[
                y * 16 : (y + 1) * 16, r * LANES : (r + 1) * LANES
            ]
    block = total[...].astype(jnp.bfloat16)
    for copy in range(ZX):
        out_ref[copy] = block


def backward_kernel(
    mine, other, phases, twist_real, twist_imag, first, second, factor_real, factor_imag,
    out_ref, half, total,
):
    weights = second[...]

    def second_block(pair, carry):
        place = pl.ds(pl.multiple_of(pair * 2 * Y, 2 * Y), 2 * Y)
        both = jnp.concatenate([mine[:, place, :], other[:, place, :]], axis=0).astype(jnp.float32)
        data = []
        for h in range(2):
            turned = both[:, h * Y : (h + 1) * Y, :].reshape(SUBGRIDS, LANES).T
            real = turned[:STRIP_COLS]
            imag = turned[STRIP_COLS:]
            fr = factor_real[pl.ds(pair * 2 + h, 1), :]
            fi = factor_imag[pl.ds(pair * 2 + h, 1), :]
            data.append(
                jnp.concatenate([real * fr + imag * fi, imag * fr - real * fi], axis=1)
            )
        data = jnp.concatenate(data, axis=0).astype(jnp.bfloat16)
        mixed = jnp.dot(data, weights, preferred_element_type=jnp.float32)
        for h in range(2):
            real = mixed[h * STRIP_COLS : (h + 1) * STRIP_COLS, :LANES]
            imag = mixed[h * STRIP_COLS : (h + 1) * STRIP_COLS, LANES:]
            tr = twist_real[pl.ds(pair * 2 + h, 1), :]
            ti = twist_imag[pl.ds(pair * 2 + h, 1), :]
            rows = pl.ds(pair * 2 + h, STRIP_COLS, stride=LINE_PITCH)
            half[0, rows, :] = real * tr + imag * ti
            half[1, rows, :] = imag * tr - real * ti
        return carry

    lax.fori_loop(0, SUB_ROWS // 2, second_block, 0, unroll=8)

    table = first[...]

    def first_block(pair, carry):
        c = pair * 2
        sums = [None] * 4
        for j in range(LAYERS):

            def column(part, h, j=j):
                start = (j * COLS + c + h) * LINE_PITCH
                return half[part, pl.ds(pl.multiple_of(start, 8), SUB_ROWS), :]

            data = jnp.concatenate(
                [
                    jnp.concatenate([column(0, 0), column(1, 0)], axis=0),
                    jnp.concatenate([column(0, 1), column(1, 1)], axis=0),
                ],
                axis=1,
            ).astype(jnp.bfloat16)
            image = jnp.dot(table, data, preferred_element_type=jnp.float32)
            for h in range(2):
                real = image[:SUB_ROWS, h * LANES : (h + 1) * LANES]
                imag = image[SUB_ROWS:, h * LANES : (h + 1) * LANES]
                rows = pl.ds(j * PHASE_ROWS + c + h, SUB_ROWS, stride=COL_PITCH)
                cosine = phases[0, rows, :]
                sine = phases[1, rows, :]
                for part, term in enumerate(
                    (real * cosine + imag * sine, imag * cosine - real * sine)
                ):
                    place = 2 * h + part
                    sums[place] = term if j == 0 else sums[place] + term
        for h in range(2):
            for part in range(2):
                total[part, pl.ds(c + h, SUB_ROWS, stride=COL_PITCH), :] = back_gain * sums[2 * h + part]
        return carry

    lax.fori_loop(0, COLS // 2, first_block, 0, unroll=4)

    def leave_block(t, carry):
        lanes = pl.ds(pl.multiple_of(t * LANES, LANES), LANES)
        for nq in range(LAYERS):
            rows = pl.ds(pl.multiple_of((nq * BLOCKS + t) * COL_PITCH, 8), COLS)
            for part in range(2):
                out_ref[nq, part, :, lanes] = total[part, rows, :].astype(jnp.bfloat16)
        return carry

    lax.fori_loop(0, BLOCKS, leave_block, 0, unroll=2)


def on_core(kernel, name, out_shape, scratch, inputs):
    is_list = isinstance(out_shape, (list, tuple))
    one = pl.BlockSpec(memory_space=pltpu.VMEM)
    return pl.pallas_call(
        kernel,
        name=name,
        out_shape=out_shape,
        in_specs=[one] * inputs,
        out_specs=[one] * len(out_shape) if is_list else one,
        scratch_shapes=list(scratch),
        compiler_params=pltpu.CompilerParams(vmem_limit_bytes=VMEM_LIMIT),
    )


def shaped(shape, kind):
    return jax.ShapeDtypeStruct(shape, kind)


def forward(pieces, factor_real, factor_imag, second):
    blocks = shaped((ZX, SUB_ROWS * Y, LANES), jnp.bfloat16)
    twist_real, twist_imag = twiddle()
    return on_core(
        forward_kernel,
        "ahead",
        [blocks, blocks, shaped((2, LAYERS * PHASE_ROWS, LANES), jnp.float32)],
        (
            pltpu.VMEM((2, PHASE_ROWS, LANES), jnp.float32),
            pltpu.VMEM((2, SUB_ROWS * LINE_PITCH, LANES), jnp.float32),
        ),
        7,
    )(pieces, twist_real, twist_imag, first_tables()[0], second, factor_real, factor_imag)


def backward(mine, other, phases, factor_real, factor_imag, second):
    twist_real, twist_imag = twiddle()
    return on_core(
        backward_kernel,
        "back",
        shaped((LAYERS, 2, COLS, QUARTER), jnp.bfloat16),
        (
            pltpu.VMEM((2, STRIP_COLS * LINE_PITCH, LANES), jnp.float32),
            pltpu.VMEM((2, PHASE_ROWS, LANES), jnp.float32),
        ),
        9,
    )(
        mine, other, phases, twist_real, twist_imag, first_tables()[1], second,
        factor_real, factor_imag,
    )


def spread(cell_index, length, kernel_taps):
    tap_count = kernel_taps.shape[0]
    offset = (jnp.arange(length, dtype=jnp.int32)[None, :] - cell_index[:, None]) % length
    wanted = (jnp.arange(tap_count, dtype=jnp.int32) - tap_count // 2) % length
    matches = (offset[:, :, None] == wanted[None, None, :]).astype(jnp.float32)
    return jnp.sum(matches * kernel_taps, axis=2)


def degrid(subgrid, row_cells, column_cells, plane, observed_vis, angle_table, kernel_taps):
    row_weights = spread(row_cells, SUB_ROWS, kernel_taps)
    column_weights = spread(column_cells, STRIP_COLS, kernel_taps)
    kernel_rows = jnp.dot(row_weights, subgrid, precision=lax.Precision.HIGHEST)
    model_real = jnp.sum(kernel_rows[:, :STRIP_COLS] * column_weights, axis=1)
    model_imag = jnp.sum(kernel_rows[:, STRIP_COLS:] * column_weights, axis=1)
    plane_pick = (plane[:, None] == jnp.arange(PLANES, dtype=jnp.int32)[None, :]).astype(
        jnp.float32
    )
    phase_angle = jnp.sum(plane_pick * angle_table[None, :], axis=1)
    cosine = jnp.cos(phase_angle)
    sine_part = jnp.sin(phase_angle)
    residual_real = observed_vis[0] - (model_real * cosine - model_imag * sine_part)
    residual_imag = observed_vis[1] - (model_real * sine_part + model_imag * cosine)
    weighted_real = residual_real * cosine + residual_imag * sine_part
    weighted_imag = residual_imag * cosine - residual_real * sine_part
    spread_cols = jnp.concatenate(
        [weighted_real[:, None] * column_weights, weighted_imag[:, None] * column_weights], axis=1
    )
    adjoint = jnp.dot(row_weights.T, spread_cols, precision=lax.Precision.HIGHEST)
    return (jnp.stack([residual_real, residual_imag]), adjoint)


def exchange(blocks, axes, groups=None):
    return lax.all_to_all(
        blocks, axes, split_axis=0, concat_axis=0, tiled=True, axis_index_groups=groups
    )


def local(
    model_strip,
    screen_angle,
    facet_window,
    facet_shift,
    kernel_taps,
    plane_angle,
    u_cell,
    v_cell,
    w_plane,
    observed,
):
    swapped = lax.axis_index("facet") % CORE == 1

    joined = jnp.concatenate(
        [
            model_strip[0].reshape(2, LAYERS, COLS, QUARTER).transpose(1, 0, 2, 3),
            screen_angle[0, 0].reshape(LAYERS, COLS, LAYERS, QUARTER).transpose(0, 2, 1, 3),
        ],
        axis=1,
    )
    pieces = exchange(joined, "layer")

    factor_real, factor_imag = facet_factor(facet_window[0], facet_shift[0], swapped)
    plain = second_tables(STAGE_ORDER)
    crossed = second_tables(np.roll(STAGE_ORDER, SUBGRIDS // CORE))
    second_ahead = jnp.where(swapped, crossed[0], plain[0])
    second_back = jnp.where(swapped, crossed[1], plain[1])
    mine, other, phases = forward(pieces, factor_real, factor_imag, second_ahead)

    arrived = lax.ppermute(other, "facet", CORE_SWAP)
    pair_sum = (mine.astype(jnp.float32) + arrived.astype(jnp.float32)).astype(jnp.bfloat16)
    plane_terms = exchange(pair_sum, "facet", PLANE_GROUPS)
    table = pack_table()
    piece = (SUB_ROWS // 4, 2 * STRIP_COLS)
    packed = on_core(
        pack_kernel,
        "pack",
        shaped((Y * LAYERS, *piece), jnp.bfloat16),
        (pltpu.VMEM((SUB_ROWS * Y, LANES), jnp.float32),),
        2,
    )(plane_terms, table)
    line_sum = jnp.sum(
        exchange(packed, ("layer", "facet"), LINE_GROUPS)
        .reshape(Y, LAYERS, *piece)
        .astype(jnp.float32),
        axis=0,
    )
    subgrid = (
        line_sum.reshape(LAYERS, SUB_ROWS // 4, 4, 2, COLS)
        .transpose(2, 1, 3, 0, 4)
        .reshape(SUB_ROWS, 2 * STRIP_COLS)
    )

    residual, adjoint = degrid(
        subgrid, u_cell[0, 0], v_cell[0, 0], w_plane[0, 0], observed[0, 0], plane_angle[0], kernel_taps
    )

    sent = (
        adjoint.astype(jnp.bfloat16)
        .reshape(4, SUB_ROWS // 4, 2, LAYERS, COLS)
        .transpose(3, 1, 0, 2, 4)
        .reshape(1, LAYERS, *piece)
    )
    line = exchange(
        jnp.broadcast_to(sent, (Y, LAYERS, *piece)).reshape(Y * LAYERS, *piece),
        ("layer", "facet"),
        LINE_GROUPS,
    )
    copies = on_core(
        unpack_kernel,
        "unpack",
        shaped((ZX, SUB_ROWS * Y, LANES), jnp.bfloat16),
        (pltpu.VMEM((SUB_ROWS * Y, LANES), jnp.float32),),
        2,
    )(line, table)
    mine_grids = exchange(copies, "facet", PLANE_GROUPS)
    other_grids = lax.ppermute(mine_grids, "facet", CORE_SWAP)
    leaving = backward(mine_grids, other_grids, phases, factor_real, factor_imag, second_back)
    gradient = (
        exchange(leaving, "layer")
        .transpose(1, 0, 2, 3)
        .reshape(1, 2, STRIP_COLS, QUARTER)
        .astype(jnp.float32)
    )
    return (residual[None, None], gradient)


def solution(mesh):
    return jax.shard_map(
        local,
        mesh=mesh,
        in_specs=(
            P("facet", None, None, "layer"),
            P("layer", "facet", None, None),
            P("facet", None),
            P("facet"),
            P(),
            P("layer", None),
            P("layer", "facet", None),
            P("layer", "facet", None),
            P("layer", "facet", None),
            P("layer", "facet", None, None),
        ),
        out_specs=(P("layer", "facet", None, None), P("facet", None, None, "layer")),
        check_vma=False,
    )
```

```python
import math

import jax
import jax.numpy as jnp
import numpy as np
from jax import lax
from jax.experimental import pallas as pl
from jax.experimental.pallas import tpu as pltpu
from jax.sharding import PartitionSpec as P

STRIP_LEN = 8192
SUB_ROWS = 64
STRIP_COLS = 64
PLANES = 8
SUBGRIDS = 128
LAYERS = 4
COLS = STRIP_COLS // LAYERS
QUARTER = STRIP_LEN // LAYERS
LANES = 128
BLOCKS = QUARTER // LANES

back_gain = 8.0

Y, Z, X, CORE = 8, 2, 4, 2
ZX = Z * X
FACET_INDEX = np.arange(SUBGRIDS).reshape(Y, Z, X, CORE)
STAGE_ORDER = FACET_INDEX.transpose(3, 1, 2, 0).reshape(-1)
PLANE_GROUPS = FACET_INDEX.transpose(0, 3, 1, 2).reshape(-1, ZX).tolist()
GLOBAL_INDEX = np.arange(LAYERS * SUBGRIDS).reshape(LAYERS, Y, Z, X, CORE)
LINE_GROUPS = GLOBAL_INDEX.transpose(2, 3, 4, 1, 0).reshape(-1, Y * LAYERS).tolist()
CORE_SWAP = [(i, i ^ 1) for i in range(SUBGRIDS)]

VMEM_LIMIT = 24 * 1024 * 1024

COL_PITCH = 24
LINE_PITCH = 72
PHASE_ROWS = SUB_ROWS * COL_PITCH


def even_series(function, degree):
    series = np.polynomial.chebyshev.Chebyshev.interpolate(
        lambda t: function(np.sqrt(np.maximum((t + 1.0) * 0.5, 0.0)) * math.pi), degree
    )
    return [float(value) for value in np.polynomial.chebyshev.cheb2poly(series.coef)]


COSINE_SERIES = even_series(np.cos, 6)
SINE_SERIES = even_series(lambda x: np.sinc(x / math.pi), 6)


def phase_parts(angle):
    t = angle * angle * (2.0 / (math.pi * math.pi)) - 1.0
    cosine = jnp.full_like(t, COSINE_SERIES[-1])
    sine = jnp.full_like(t, SINE_SERIES[-1])
    for value in COSINE_SERIES[-2::-1]:
        cosine = cosine * t + value
    for value in SINE_SERIES[-2::-1]:
        sine = sine * t + value
    return cosine, sine * angle


def fourier_table(rows, length):
    turn_count = rows[:, None] * np.arange(length)[None, :] % length
    angles = 2.0 * math.pi / length * turn_count
    table = np.stack([np.cos(angles), -np.sin(angles)]) / math.sqrt(length)
    return table.astype(np.float32).astype(jnp.bfloat16)


def twiddle():
    turn_count = np.arange(SUB_ROWS)[:, None] * np.arange(LANES)[None, :] % STRIP_LEN
    angles = 2.0 * math.pi / STRIP_LEN * turn_count
    return (np.cos(angles).astype(np.float32), (-np.sin(angles)).astype(np.float32))


def first_tables():
    real, imag = fourier_table(np.arange(SUB_ROWS), SUB_ROWS)
    ahead = np.block([[real, -imag], [imag, real]])
    back = np.block([[real.T, imag.T], [-imag.T, real.T]])
    return (ahead, back)


def second_tables(order):
    real, imag = fourier_table(order, SUBGRIDS)
    ahead = np.block([[real.T, imag.T], [-imag.T, real.T]])
    back = np.block([[real, -imag], [imag, real]])
    return (ahead, back)


def pack_table():
    table = np.zeros((4, 2, LAYERS, COLS, LAYERS, 4, 2, COLS), np.float32)
    for r in range(4):
        for p in range(2):
            for layer in range(LAYERS):
                for c in range(COLS):
                    table[r, p, layer, c, layer, r, p, c] = 1.0
    return table.reshape(4 * LANES, 4 * LANES).astype(jnp.bfloat16)


def facet_factor(window, shift_cells, swapped):
    def staged(values):
        ordered = values.reshape(Y, Z, X, CORE, SUB_ROWS).transpose(4, 3, 1, 2, 0)
        mine = ordered.reshape(SUB_ROWS, CORE, SUBGRIDS // CORE)
        return jnp.where(swapped, mine[:, ::-1], mine).reshape(SUB_ROWS, SUBGRIDS)

    positions = jnp.arange(STRIP_LEN, dtype=jnp.int32)
    turn_count = positions * shift_cells % STRIP_LEN
    angles = 2.0 * math.pi / STRIP_LEN * turn_count.astype(jnp.float32)
    return (staged(window * jnp.cos(angles)), staged(-window * jnp.sin(angles)))


def gather_kernel(strip, screen, out_ref, sems):
    copies = []
    for cq in range(LAYERS):
        rows = pl.ds(cq * COLS, COLS)
        pairs = [(strip.at[part, rows, :], part) for part in range(2)]
        pairs += [
            (screen.at[rows, pl.ds(nq * QUARTER, QUARTER)], 2 + nq) for nq in range(LAYERS)
        ]
        for source, place in pairs:
            copies.append(
                pltpu.make_async_copy(source, out_ref.at[cq, place], sems.at[len(copies)])
            )
    for copy in copies:
        copy.start()
    for copy in copies:
        copy.wait()


def phase_copy(source, target, sems, layer):
    rows = pl.ds(layer * PHASE_ROWS, PHASE_ROWS)
    return pltpu.make_async_copy(source.at[:, rows, :], target.at[:, rows, :], sems.at[layer])


def forward_kernel(
    pieces, twist_real, twist_imag, first, second, factor_real, factor_imag,
    mine_ref, other_ref, phases_out, phases, strip, half, sems,
):
    table = first[...]

    def strip_block(t, carry):
        lanes = pl.ds(pl.multiple_of(t * LANES, LANES), LANES)
        for nq in range(LAYERS):
            rows = pl.ds(pl.multiple_of((nq * BLOCKS + t) * COL_PITCH, 8), COLS)
            for part in range(2):
                strip[part, rows, :] = pieces[nq, part, :, lanes].astype(jnp.float32)
        return carry

    lax.fori_loop(0, BLOCKS, strip_block, 0, unroll=2)
    for layer in range(LAYERS):

        def phase_block(t, carry, layer=layer):
            lanes = pl.ds(pl.multiple_of(t * LANES, LANES), LANES)
            for nq in range(LAYERS):
                cosine, sine = phase_parts(pieces[layer, 2 + nq, :, lanes].astype(jnp.float32))
                rows = pl.ds(
                    pl.multiple_of(layer * PHASE_ROWS + (nq * BLOCKS + t) * COL_PITCH, 8), COLS
                )
                phases[0, rows, :] = cosine
                phases[1, rows, :] = sine
            return carry

        lax.fori_loop(0, BLOCKS, phase_block, 0, unroll=4)
        phase_copy(phases, phases_out, sems, layer).start()

        def first_block(pair, carry, layer=layer):
            c = pair * 2
            data = []
            for h in range(2):
                column = pl.ds(c + h, SUB_ROWS, stride=COL_PITCH)
                turn = pl.ds(layer * PHASE_ROWS + c + h, SUB_ROWS, stride=COL_PITCH)
                real, imag = strip[0, column, :], strip[1, column, :]
                cosine, sine = phases[0, turn, :], phases[1, turn, :]
                data.append(
                    jnp.concatenate(
                        [real * cosine - imag * sine, real * sine + imag * cosine], axis=0
                    )
                )
            data = jnp.concatenate(data, axis=1).astype(jnp.bfloat16)
            mixed = jnp.dot(table, data, preferred_element_type=jnp.float32)
            for h in range(2):
                real = mixed[:SUB_ROWS, h * LANES : (h + 1) * LANES]
                imag = mixed[SUB_ROWS:, h * LANES : (h + 1) * LANES]
                rows = pl.ds(layer * COLS + c + h, SUB_ROWS, stride=LINE_PITCH)
                half[0, rows, :] = real * twist_real[...] - imag * twist_imag[...]
                half[1, rows, :] = real * twist_imag[...] + imag * twist_real[...]
            return carry

        lax.fori_loop(0, COLS // 2, first_block, 0, unroll=4)

    weights = second[...]

    def second_block(pair, carry):
        data = []
        for h in range(2):
            rows = pl.ds(pl.multiple_of((pair * 2 + h) * LINE_PITCH, 8), STRIP_COLS)
            data.append(jnp.concatenate([half[0, rows, :], half[1, rows, :]], axis=1))
        data = jnp.concatenate(data, axis=0).astype(jnp.bfloat16)
        spectrum = jnp.dot(data, weights, preferred_element_type=jnp.float32)
        blocks = []
        for h in range(2):
            real = spectrum[h * STRIP_COLS : (h + 1) * STRIP_COLS, :LANES]
            imag = spectrum[h * STRIP_COLS : (h + 1) * STRIP_COLS, LANES:]
            fr = factor_real[pl.ds(pair * 2 + h, 1), :]
            fi = factor_imag[pl.ds(pair * 2 + h, 1), :]
            turned = jnp.concatenate([real * fr - imag * fi, real * fi + imag * fr], axis=0).T
            blocks.append(turned.reshape(CORE * ZX, Y, LANES))
        both = jnp.concatenate(blocks, axis=1).astype(jnp.bfloat16)
        place = pl.ds(pl.multiple_of(pair * 2 * Y, 2 * Y), 2 * Y)
        mine_ref[:, place, :] = both[:ZX]
        other_ref[:, place, :] = both[ZX:]
        return carry

    lax.fori_loop(0, SUB_ROWS // 2, second_block, 0, unroll=8)
    for layer in range(LAYERS):
        phase_copy(phases, phases_out, sems, layer).wait()


def pack_kernel(pieces, table, out_ref, total):
    total[...] = jnp.sum(pieces[...].astype(jnp.float32), axis=0)
    rows = []
    for y in range(Y):
        block = total[pl.ds(y, SUB_ROWS, stride=Y), :]
        rows.append(jnp.concatenate([block[r * 16 : (r + 1) * 16] for r in range(4)], axis=1))
    data = jnp.concatenate(rows, axis=0).astype(jnp.bfloat16)
    packed = jnp.dot(data, table[...], preferred_element_type=jnp.float32).astype(jnp.bfloat16)
    for y in range(Y):
        for layer in range(LAYERS):
            out_ref[y * LAYERS + layer] = packed[
                y * 16 : (y + 1) * 16, layer * LANES : (layer + 1) * LANES
            ]


def unpack_kernel(line, table, out_ref, total):
    data = jnp.concatenate(
        [
            jnp.concatenate([line[y * LAYERS + layer] for layer in range(LAYERS)], axis=1)
            for y in range(Y)
        ],
        axis=0,
    )
    grids = lax.dot_general(
        data, table[...], (((1,), (1,)), ((), ())), preferred_element_type=jnp.float32
    )
    for y in range(Y):
        for r in range(4):
            total[pl.ds(r * 16 * Y + y, 16, stride=Y), :] = grids[
                y * 16 : (y + 1) * 16, r * LANES : (r + 1) * LANES
            ]
    block = total[...].astype(jnp.bfloat16)
    for copy in range(ZX):
        out_ref[copy] = block


def backward_kernel(
    mine, other, phases_in, twist_real, twist_imag, first, second, factor_real, factor_imag,
    out_ref, phases, half, total, sems,
):
    for layer in range(LAYERS):
        phase_copy(phases_in, phases, sems, layer).start()
    weights = second[...]

    def second_block(pair, carry):
        place = pl.ds(pl.multiple_of(pair * 2 * Y, 2 * Y), 2 * Y)
        both = jnp.concatenate([mine[:, place, :], other[:, place, :]], axis=0).astype(jnp.float32)
        data = []
        for h in range(2):
            turned = both[:, h * Y : (h + 1) * Y, :].reshape(SUBGRIDS, LANES).T
            real = turned[:STRIP_COLS]
            imag = turned[STRIP_COLS:]
            fr = factor_real[pl.ds(pair * 2 + h, 1), :]
            fi = factor_imag[pl.ds(pair * 2 + h, 1), :]
            data.append(
                jnp.concatenate([real * fr + imag * fi, imag * fr - real * fi], axis=1)
            )
        data = jnp.concatenate(data, axis=0).astype(jnp.bfloat16)
        mixed = jnp.dot(data, weights, preferred_element_type=jnp.float32)
        for h in range(2):
            real = mixed[h * STRIP_COLS : (h + 1) * STRIP_COLS, :LANES]
            imag = mixed[h * STRIP_COLS : (h + 1) * STRIP_COLS, LANES:]
            tr = twist_real[pl.ds(pair * 2 + h, 1), :]
            ti = twist_imag[pl.ds(pair * 2 + h, 1), :]
            rows = pl.ds(pair * 2 + h, STRIP_COLS, stride=LINE_PITCH)
            half[0, rows, :] = real * tr + imag * ti
            half[1, rows, :] = imag * tr - real * ti
        return carry

    lax.fori_loop(0, SUB_ROWS // 2, second_block, 0, unroll=8)

    for layer in range(LAYERS):
        phase_copy(phases_in, phases, sems, layer).wait()
    table = first[...]

    def first_block(pair, carry):
        c = pair * 2
        sums = [None] * 4
        for j in range(LAYERS):

            def column(part, h, j=j):
                start = (j * COLS + c + h) * LINE_PITCH
                return half[part, pl.ds(pl.multiple_of(start, 8), SUB_ROWS), :]

            data = jnp.concatenate(
                [
                    jnp.concatenate([column(0, 0), column(1, 0)], axis=0),
                    jnp.concatenate([column(0, 1), column(1, 1)], axis=0),
                ],
                axis=1,
            ).astype(jnp.bfloat16)
            image = jnp.dot(table, data, preferred_element_type=jnp.float32)
            for h in range(2):
                real = image[:SUB_ROWS, h * LANES : (h + 1) * LANES]
                imag = image[SUB_ROWS:, h * LANES : (h + 1) * LANES]
                rows = pl.ds(j * PHASE_ROWS + c + h, SUB_ROWS, stride=COL_PITCH)
                cosine = phases[0, rows, :]
                sine = phases[1, rows, :]
                for part, term in enumerate(
                    (real * cosine + imag * sine, imag * cosine - real * sine)
                ):
                    place = 2 * h + part
                    sums[place] = term if j == 0 else sums[place] + term
        for h in range(2):
            for part in range(2):
                total[part, pl.ds(c + h, SUB_ROWS, stride=COL_PITCH), :] = back_gain * sums[2 * h + part]
        return carry

    lax.fori_loop(0, COLS // 2, first_block, 0, unroll=4)

    def leave_block(t, carry):
        lanes = pl.ds(pl.multiple_of(t * LANES, LANES), LANES)
        for nq in range(LAYERS):
            rows = pl.ds(pl.multiple_of((nq * BLOCKS + t) * COL_PITCH, 8), COLS)
            for part in range(2):
                out_ref[nq, part, :, lanes] = total[part, rows, :].astype(jnp.bfloat16)
        return carry

    lax.fori_loop(0, BLOCKS, leave_block, 0, unroll=2)


def on_core(kernel, name, out_shape, scratch, inputs, far_in=(), far_out=()):
    near, far = pl.BlockSpec(memory_space=pltpu.VMEM), pl.BlockSpec(memory_space=pltpu.HBM)
    return pl.pallas_call(
        kernel,
        name=name,
        out_shape=out_shape,
        in_specs=[far if i in far_in else near for i in range(inputs)],
        out_specs=[far if i in far_out else near for i in range(len(out_shape))],
        scratch_shapes=list(scratch),
        compiler_params=pltpu.CompilerParams(vmem_limit_bytes=VMEM_LIMIT),
    )


def shaped(shape, kind):
    return jax.ShapeDtypeStruct(shape, kind)


def far(values):
    return pltpu.with_memory_space_constraint(values, pltpu.HBM)


def gather(strip, screen):
    blocks = shaped((LAYERS, 2 + LAYERS, COLS, QUARTER), jnp.bfloat16)
    sems = pltpu.SemaphoreType.DMA((LAYERS * (2 + LAYERS),))
    return on_core(gather_kernel, "gather", [blocks], (sems,), 2, (0, 1), (0,))(
        far(strip), far(screen)
    )[0]


def forward(pieces, factor_real, factor_imag, second):
    blocks = shaped((ZX, SUB_ROWS * Y, LANES), jnp.bfloat16)
    phases = (2, LAYERS * PHASE_ROWS, LANES)
    twist_real, twist_imag = twiddle()
    return on_core(
        forward_kernel,
        "ahead",
        [blocks, blocks, pltpu.HBM(phases, jnp.float32)],
        (
            pltpu.VMEM(phases, jnp.float32),
            pltpu.VMEM((2, PHASE_ROWS, LANES), jnp.float32),
            pltpu.VMEM((2, SUB_ROWS * LINE_PITCH, LANES), jnp.float32),
            pltpu.SemaphoreType.DMA((LAYERS,)),
        ),
        7,
        far_out=(2,),
    )(pieces, twist_real, twist_imag, first_tables()[0], second, factor_real, factor_imag)


def backward(mine, other, phases, factor_real, factor_imag, second):
    twist_real, twist_imag = twiddle()
    return on_core(
        backward_kernel,
        "back",
        [shaped((LAYERS, 2, COLS, QUARTER), jnp.bfloat16)],
        (
            pltpu.VMEM((2, LAYERS * PHASE_ROWS, LANES), jnp.float32),
            pltpu.VMEM((2, STRIP_COLS * LINE_PITCH, LANES), jnp.float32),
            pltpu.VMEM((2, PHASE_ROWS, LANES), jnp.float32),
            pltpu.SemaphoreType.DMA((LAYERS,)),
        ),
        9,
        far_in=(2,),
    )(
        mine, other, far(phases), twist_real, twist_imag, first_tables()[1], second,
        factor_real, factor_imag,
    )[0]


def spread(cell_index, length, kernel_taps):
    tap_count = kernel_taps.shape[0]
    offset = (jnp.arange(length, dtype=jnp.int32)[None, :] - cell_index[:, None]) % length
    wanted = (jnp.arange(tap_count, dtype=jnp.int32) - tap_count // 2) % length
    matches = (offset[:, :, None] == wanted[None, None, :]).astype(jnp.float32)
    return jnp.sum(matches * kernel_taps, axis=2)


def degrid(subgrid, row_cells, column_cells, plane, observed_vis, angle_table, kernel_taps):
    row_weights = spread(row_cells, SUB_ROWS, kernel_taps)
    column_weights = spread(column_cells, STRIP_COLS, kernel_taps)
    kernel_rows = jnp.dot(row_weights, subgrid, precision=lax.Precision.HIGHEST)
    model_real = jnp.sum(kernel_rows[:, :STRIP_COLS] * column_weights, axis=1)
    model_imag = jnp.sum(kernel_rows[:, STRIP_COLS:] * column_weights, axis=1)
    plane_pick = (plane[:, None] == jnp.arange(PLANES, dtype=jnp.int32)[None, :]).astype(
        jnp.float32
    )
    phase_angle = jnp.sum(plane_pick * angle_table[None, :], axis=1)
    cosine = jnp.cos(phase_angle)
    sine_part = jnp.sin(phase_angle)
    residual_real = observed_vis[0] - (model_real * cosine - model_imag * sine_part)
    residual_imag = observed_vis[1] - (model_real * sine_part + model_imag * cosine)
    weighted_real = residual_real * cosine + residual_imag * sine_part
    weighted_imag = residual_imag * cosine - residual_real * sine_part
    spread_cols = jnp.concatenate(
        [weighted_real[:, None] * column_weights, weighted_imag[:, None] * column_weights], axis=1
    )
    adjoint = jnp.dot(row_weights.T, spread_cols, precision=lax.Precision.HIGHEST)
    return (jnp.stack([residual_real, residual_imag]), adjoint)


def exchange(blocks, axes, groups=None):
    return lax.all_to_all(
        blocks, axes, split_axis=0, concat_axis=0, tiled=True, axis_index_groups=groups
    )


def local(
    model_strip,
    screen_angle,
    facet_window,
    facet_shift,
    kernel_taps,
    plane_angle,
    u_cell,
    v_cell,
    w_plane,
    observed,
):
    swapped = lax.axis_index("facet") % CORE == 1

    pieces = exchange(gather(model_strip[0], screen_angle[0, 0]), "layer")

    factor_real, factor_imag = facet_factor(facet_window[0], facet_shift[0], swapped)
    plain = second_tables(STAGE_ORDER)
    crossed = second_tables(np.roll(STAGE_ORDER, SUBGRIDS // CORE))
    second_ahead = jnp.where(swapped, crossed[0], plain[0])
    second_back = jnp.where(swapped, crossed[1], plain[1])
    mine, other, phases = forward(pieces, factor_real, factor_imag, second_ahead)

    arrived = lax.ppermute(other, "facet", CORE_SWAP)
    pair_sum = (mine.astype(jnp.float32) + arrived.astype(jnp.float32)).astype(jnp.bfloat16)
    plane_terms = exchange(pair_sum, "facet", PLANE_GROUPS)
    table = pack_table()
    piece = (SUB_ROWS // 4, 2 * STRIP_COLS)
    packed = on_core(
        pack_kernel,
        "pack",
        [shaped((Y * LAYERS, *piece), jnp.bfloat16)],
        (pltpu.VMEM((SUB_ROWS * Y, LANES), jnp.float32),),
        2,
    )(plane_terms, table)[0]
    line_sum = jnp.sum(
        exchange(packed, ("layer", "facet"), LINE_GROUPS)
        .reshape(Y, LAYERS, *piece)
        .astype(jnp.float32),
        axis=0,
    )
    subgrid = (
        line_sum.reshape(LAYERS, SUB_ROWS // 4, 4, 2, COLS)
        .transpose(2, 1, 3, 0, 4)
        .reshape(SUB_ROWS, 2 * STRIP_COLS)
    )

    residual, adjoint = degrid(
        subgrid, u_cell[0, 0], v_cell[0, 0], w_plane[0, 0], observed[0, 0], plane_angle[0], kernel_taps
    )

    sent = (
        adjoint.astype(jnp.bfloat16)
        .reshape(4, SUB_ROWS // 4, 2, LAYERS, COLS)
        .transpose(3, 1, 0, 2, 4)
        .reshape(1, LAYERS, *piece)
    )
    line = exchange(
        jnp.broadcast_to(sent, (Y, LAYERS, *piece)).reshape(Y * LAYERS, *piece),
        ("layer", "facet"),
        LINE_GROUPS,
    )
    copies = on_core(
        unpack_kernel,
        "unpack",
        [shaped((ZX, SUB_ROWS * Y, LANES), jnp.bfloat16)],
        (pltpu.VMEM((SUB_ROWS * Y, LANES), jnp.float32),),
        2,
    )(line, table)[0]
    mine_grids = exchange(copies, "facet", PLANE_GROUPS)
    other_grids = lax.ppermute(mine_grids, "facet", CORE_SWAP)
    leaving = backward(mine_grids, other_grids, phases, factor_real, factor_imag, second_back)
    gradient = (
        exchange(leaving, "layer")
        .transpose(1, 0, 2, 3)
        .reshape(1, 2, STRIP_COLS, QUARTER)
        .astype(jnp.float32)
    )
    return (residual[None, None], gradient)


def solution(mesh):
    return jax.shard_map(
        local,
        mesh=mesh,
        in_specs=(
            P("facet", None, None, "layer"),
            P("layer", "facet", None, None),
            P("facet", None),
            P("facet"),
            P(),
            P("layer", None),
            P("layer", "facet", None),
            P("layer", "facet", None),
            P("layer", "facet", None),
            P("layer", "facet", None, None),
        ),
        out_specs=(P("layer", "facet", None, None), P("facet", None, None, "layer")),
        check_vma=False,
    )
```

```python
import math

import jax
import jax.numpy as jnp
import numpy as np
from jax import lax
from jax.experimental import pallas as pl
from jax.experimental.pallas import tpu as pltpu
from jax.sharding import PartitionSpec as P

STRIP_LEN = 8192
SUB_ROWS = 64
STRIP_COLS = 64
PLANES = 8
SUBGRIDS = 128
LAYERS = 4
COLS = STRIP_COLS // LAYERS
QUARTER = STRIP_LEN // LAYERS
LANES = 128
BLOCKS = QUARTER // LANES

back_gain = 8.0

Y, Z, X, CORE = 8, 2, 4, 2
ZX = Z * X
FACET_INDEX = np.arange(SUBGRIDS).reshape(Y, Z, X, CORE)
STAGE_ORDER = FACET_INDEX.transpose(3, 1, 2, 0).reshape(-1)
PLANE_GROUPS = FACET_INDEX.transpose(0, 3, 1, 2).reshape(-1, ZX).tolist()
GLOBAL_INDEX = np.arange(LAYERS * SUBGRIDS).reshape(LAYERS, Y, Z, X, CORE)
LINE_GROUPS = GLOBAL_INDEX.transpose(2, 3, 4, 1, 0).reshape(-1, Y * LAYERS).tolist()
CORE_SWAP = [(i, i ^ 1) for i in range(SUBGRIDS)]

VMEM_LIMIT = 24 * 1024 * 1024

COL_PITCH = 24
LINE_PITCH = 72
PHASE_ROWS = SUB_ROWS * COL_PITCH


def even_series(function, degree):
    series = np.polynomial.chebyshev.Chebyshev.interpolate(
        lambda t: function(np.sqrt(np.maximum((t + 1.0) * 0.5, 0.0)) * math.pi), degree
    )
    return [float(value) for value in np.polynomial.chebyshev.cheb2poly(series.coef)]


COSINE_SERIES = even_series(np.cos, 6)
SINE_SERIES = even_series(lambda x: np.sinc(x / math.pi), 6)


def phase_parts(angle):
    t = angle * angle * (2.0 / (math.pi * math.pi)) - 1.0
    cosine = jnp.full_like(t, COSINE_SERIES[-1])
    sine = jnp.full_like(t, SINE_SERIES[-1])
    for value in COSINE_SERIES[-2::-1]:
        cosine = cosine * t + value
    for value in SINE_SERIES[-2::-1]:
        sine = sine * t + value
    return cosine, sine * angle


def fourier_table(rows, length):
    turn_count = rows[:, None] * np.arange(length)[None, :] % length
    angles = 2.0 * math.pi / length * turn_count
    table = np.stack([np.cos(angles), -np.sin(angles)]) / math.sqrt(length)
    return table.astype(np.float32).astype(jnp.bfloat16)


def twiddle():
    turn_count = np.arange(SUB_ROWS)[:, None] * np.arange(LANES)[None, :] % STRIP_LEN
    angles = 2.0 * math.pi / STRIP_LEN * turn_count
    return (np.cos(angles).astype(np.float32), (-np.sin(angles)).astype(np.float32))


def first_tables():
    real, imag = fourier_table(np.arange(SUB_ROWS), SUB_ROWS)
    ahead = np.block([[real, -imag], [imag, real]])
    back = np.block([[real.T, imag.T], [-imag.T, real.T]])
    return (ahead, back)


def second_tables(order):
    real, imag = fourier_table(order, SUBGRIDS)
    ahead = np.block([[real.T, imag.T], [-imag.T, real.T]])
    back = np.block([[real, -imag], [imag, real]])
    return (ahead, back)


def pack_table():
    table = np.zeros((4, 2, LAYERS, COLS, LAYERS, 4, 2, COLS), np.float32)
    for r in range(4):
        for p in range(2):
            for layer in range(LAYERS):
                for c in range(COLS):
                    table[r, p, layer, c, layer, r, p, c] = 1.0
    return table.reshape(4 * LANES, 4 * LANES).astype(jnp.bfloat16)


def facet_factor(window, shift_cells, swapped):
    def staged(values):
        ordered = values.reshape(Y, Z, X, CORE, SUB_ROWS).transpose(4, 3, 1, 2, 0)
        mine = ordered.reshape(SUB_ROWS, CORE, SUBGRIDS // CORE)
        return jnp.where(swapped, mine[:, ::-1], mine).reshape(SUB_ROWS, SUBGRIDS)

    positions = jnp.arange(STRIP_LEN, dtype=jnp.int32)
    turn_count = positions * shift_cells % STRIP_LEN
    angles = 2.0 * math.pi / STRIP_LEN * turn_count.astype(jnp.float32)
    return (staged(window * jnp.cos(angles)), staged(-window * jnp.sin(angles)))


def gather_kernel(strip, screen, out_ref, blocks, in_sems, out_sems):
    def arrivals(cq):
        rows = pl.ds(cq * COLS, COLS)
        pairs = [(strip.at[:, rows, :], blocks.at[cq, pl.ds(0, 2)])]
        for nq in range(LAYERS):
            pairs.append(
                (screen.at[rows, pl.ds(nq * QUARTER, QUARTER)], blocks.at[cq, 2 + nq])
            )
        return [
            pltpu.make_async_copy(source, target, in_sems.at[cq, i])
            for i, (source, target) in enumerate(pairs)
        ]

    def departure(cq):
        return pltpu.make_async_copy(blocks.at[cq], out_ref.at[cq], out_sems.at[cq])

    for cq in range(LAYERS):
        for copy in arrivals(cq):
            copy.start()
    for cq in range(LAYERS):
        for copy in arrivals(cq):
            copy.wait()
        departure(cq).start()
    for cq in range(LAYERS):
        departure(cq).wait()


def phase_copy(source, target, sems, layer):
    rows = pl.ds(layer * PHASE_ROWS, PHASE_ROWS)
    return pltpu.make_async_copy(source.at[:, rows, :], target.at[:, rows, :], sems.at[layer])


def forward_kernel(
    pieces, twist_real, twist_imag, first, second, factor_real, factor_imag,
    mine_ref, other_ref, phases_out, phases, strip, half, sems,
):
    table = first[...]

    def strip_block(t, carry):
        lanes = pl.ds(pl.multiple_of(t * LANES, LANES), LANES)
        for nq in range(LAYERS):
            rows = pl.ds(pl.multiple_of((nq * BLOCKS + t) * COL_PITCH, 8), COLS)
            for part in range(2):
                strip[part, rows, :] = pieces[nq, part, :, lanes].astype(jnp.float32)
        return carry

    lax.fori_loop(0, BLOCKS, strip_block, 0, unroll=2)
    for layer in range(LAYERS):

        def phase_block(t, carry, layer=layer):
            lanes = pl.ds(pl.multiple_of(t * LANES, LANES), LANES)
            for nq in range(LAYERS):
                cosine, sine = phase_parts(pieces[layer, 2 + nq, :, lanes].astype(jnp.float32))
                rows = pl.ds(
                    pl.multiple_of(layer * PHASE_ROWS + (nq * BLOCKS + t) * COL_PITCH, 8), COLS
                )
                phases[0, rows, :] = cosine
                phases[1, rows, :] = sine
            return carry

        lax.fori_loop(0, BLOCKS, phase_block, 0, unroll=4)
        phase_copy(phases, phases_out, sems, layer).start()

        def first_block(pair, carry, layer=layer):
            c = pair * 2
            data = []
            for h in range(2):
                column = pl.ds(c + h, SUB_ROWS, stride=COL_PITCH)
                turn = pl.ds(layer * PHASE_ROWS + c + h, SUB_ROWS, stride=COL_PITCH)
                real, imag = strip[0, column, :], strip[1, column, :]
                cosine, sine = phases[0, turn, :], phases[1, turn, :]
                data.append(
                    jnp.concatenate(
                        [real * cosine - imag * sine, real * sine + imag * cosine], axis=0
                    )
                )
            data = jnp.concatenate(data, axis=1).astype(jnp.bfloat16)
            mixed = jnp.dot(table, data, preferred_element_type=jnp.float32)
            for h in range(2):
                real = mixed[:SUB_ROWS, h * LANES : (h + 1) * LANES]
                imag = mixed[SUB_ROWS:, h * LANES : (h + 1) * LANES]
                rows = pl.ds(layer * COLS + c + h, SUB_ROWS, stride=LINE_PITCH)
                half[0, rows, :] = real * twist_real[...] - imag * twist_imag[...]
                half[1, rows, :] = real * twist_imag[...] + imag * twist_real[...]
            return carry

        lax.fori_loop(0, COLS // 2, first_block, 0, unroll=4)

    weights = second[...]

    def second_block(pair, carry):
        data = []
        for h in range(2):
            rows = pl.ds(pl.multiple_of((pair * 2 + h) * LINE_PITCH, 8), STRIP_COLS)
            data.append(jnp.concatenate([half[0, rows, :], half[1, rows, :]], axis=1))
        data = jnp.concatenate(data, axis=0).astype(jnp.bfloat16)
        spectrum = jnp.dot(data, weights, preferred_element_type=jnp.float32)
        blocks = []
        for h in range(2):
            real = spectrum[h * STRIP_COLS : (h + 1) * STRIP_COLS, :LANES]
            imag = spectrum[h * STRIP_COLS : (h + 1) * STRIP_COLS, LANES:]
            fr = factor_real[pl.ds(pair * 2 + h, 1), :]
            fi = factor_imag[pl.ds(pair * 2 + h, 1), :]
            turned = jnp.concatenate([real * fr - imag * fi, real * fi + imag * fr], axis=0).T
            blocks.append(turned.reshape(CORE * ZX, Y, LANES))
        both = jnp.concatenate(blocks, axis=1).astype(jnp.bfloat16)
        place = pl.ds(pl.multiple_of(pair * 2 * Y, 2 * Y), 2 * Y)
        mine_ref[:, place, :] = both[:ZX]
        other_ref[:, place, :] = both[ZX:]
        return carry

    lax.fori_loop(0, SUB_ROWS // 2, second_block, 0, unroll=8)
    for layer in range(LAYERS):
        phase_copy(phases, phases_out, sems, layer).wait()


def pack_kernel(pieces, table, out_ref, total):
    total[...] = jnp.sum(pieces[...].astype(jnp.float32), axis=0)
    rows = []
    for y in range(Y):
        block = total[pl.ds(y, SUB_ROWS, stride=Y), :]
        rows.append(jnp.concatenate([block[r * 16 : (r + 1) * 16] for r in range(4)], axis=1))
    data = jnp.concatenate(rows, axis=0).astype(jnp.bfloat16)
    packed = jnp.dot(data, table[...], preferred_element_type=jnp.float32).astype(jnp.bfloat16)
    for y in range(Y):
        for layer in range(LAYERS):
            out_ref[y * LAYERS + layer] = packed[
                y * 16 : (y + 1) * 16, layer * LANES : (layer + 1) * LANES
            ]


def unpack_kernel(line, table, out_ref, total):
    data = jnp.concatenate(
        [
            jnp.concatenate([line[y * LAYERS + layer] for layer in range(LAYERS)], axis=1)
            for y in range(Y)
        ],
        axis=0,
    )
    grids = lax.dot_general(
        data, table[...], (((1,), (1,)), ((), ())), preferred_element_type=jnp.float32
    )
    for y in range(Y):
        for r in range(4):
            total[pl.ds(r * 16 * Y + y, 16, stride=Y), :] = grids[
                y * 16 : (y + 1) * 16, r * LANES : (r + 1) * LANES
            ]
    block = total[...].astype(jnp.bfloat16)
    for copy in range(ZX):
        out_ref[copy] = block


def backward_kernel(
    mine, other, phases_in, twist_real, twist_imag, first, second, factor_real, factor_imag,
    out_ref, phases, half, total, sems,
):
    for layer in range(LAYERS):
        phase_copy(phases_in, phases, sems, layer).start()
    weights = second[...]

    def second_block(pair, carry):
        place = pl.ds(pl.multiple_of(pair * 2 * Y, 2 * Y), 2 * Y)
        both = jnp.concatenate([mine[:, place, :], other[:, place, :]], axis=0).astype(jnp.float32)
        data = []
        for h in range(2):
            turned = both[:, h * Y : (h + 1) * Y, :].reshape(SUBGRIDS, LANES).T
            real = turned[:STRIP_COLS]
            imag = turned[STRIP_COLS:]
            fr = factor_real[pl.ds(pair * 2 + h, 1), :]
            fi = factor_imag[pl.ds(pair * 2 + h, 1), :]
            data.append(
                jnp.concatenate([real * fr + imag * fi, imag * fr - real * fi], axis=1)
            )
        data = jnp.concatenate(data, axis=0).astype(jnp.bfloat16)
        mixed = jnp.dot(data, weights, preferred_element_type=jnp.float32)
        for h in range(2):
            real = mixed[h * STRIP_COLS : (h + 1) * STRIP_COLS, :LANES]
            imag = mixed[h * STRIP_COLS : (h + 1) * STRIP_COLS, LANES:]
            tr = twist_real[pl.ds(pair * 2 + h, 1), :]
            ti = twist_imag[pl.ds(pair * 2 + h, 1), :]
            rows = pl.ds(pair * 2 + h, STRIP_COLS, stride=LINE_PITCH)
            half[0, rows, :] = real * tr + imag * ti
            half[1, rows, :] = imag * tr - real * ti
        return carry

    lax.fori_loop(0, SUB_ROWS // 2, second_block, 0, unroll=8)

    for layer in range(LAYERS):
        phase_copy(phases_in, phases, sems, layer).wait()
    table = first[...]

    def first_block(pair, carry):
        c = pair * 2
        sums = [None] * 4
        for j in range(LAYERS):

            def column(part, h, j=j):
                start = (j * COLS + c + h) * LINE_PITCH
                return half[part, pl.ds(pl.multiple_of(start, 8), SUB_ROWS), :]

            data = jnp.concatenate(
                [
                    jnp.concatenate([column(0, 0), column(1, 0)], axis=0),
                    jnp.concatenate([column(0, 1), column(1, 1)], axis=0),
                ],
                axis=1,
            ).astype(jnp.bfloat16)
            image = jnp.dot(table, data, preferred_element_type=jnp.float32)
            for h in range(2):
                real = image[:SUB_ROWS, h * LANES : (h + 1) * LANES]
                imag = image[SUB_ROWS:, h * LANES : (h + 1) * LANES]
                rows = pl.ds(j * PHASE_ROWS + c + h, SUB_ROWS, stride=COL_PITCH)
                cosine = phases[0, rows, :]
                sine = phases[1, rows, :]
                for part, term in enumerate(
                    (real * cosine + imag * sine, imag * cosine - real * sine)
                ):
                    place = 2 * h + part
                    sums[place] = term if j == 0 else sums[place] + term
        for h in range(2):
            for part in range(2):
                total[part, pl.ds(c + h, SUB_ROWS, stride=COL_PITCH), :] = back_gain * sums[2 * h + part]
        return carry

    lax.fori_loop(0, COLS // 2, first_block, 0, unroll=4)

    def leave_block(t, carry):
        lanes = pl.ds(pl.multiple_of(t * LANES, LANES), LANES)
        for nq in range(LAYERS):
            rows = pl.ds(pl.multiple_of((nq * BLOCKS + t) * COL_PITCH, 8), COLS)
            for part in range(2):
                out_ref[nq, part, :, lanes] = total[part, rows, :].astype(jnp.bfloat16)
        return carry

    lax.fori_loop(0, BLOCKS, leave_block, 0, unroll=2)


def on_core(kernel, name, out_shape, scratch, inputs, far_in=(), far_out=()):
    near, far = pl.BlockSpec(memory_space=pltpu.VMEM), pl.BlockSpec(memory_space=pltpu.HBM)
    return pl.pallas_call(
        kernel,
        name=name,
        out_shape=out_shape,
        in_specs=[far if i in far_in else near for i in range(inputs)],
        out_specs=[far if i in far_out else near for i in range(len(out_shape))],
        scratch_shapes=list(scratch),
        compiler_params=pltpu.CompilerParams(vmem_limit_bytes=VMEM_LIMIT),
    )


def shaped(shape, kind):
    return jax.ShapeDtypeStruct(shape, kind)


def far(values):
    return pltpu.with_memory_space_constraint(values, pltpu.HBM)


def gather(strip, screen):
    blocks = (LAYERS, 2 + LAYERS, COLS, QUARTER)
    return on_core(
        gather_kernel,
        "gather",
        [pltpu.HBM(blocks, jnp.bfloat16)],
        (
            pltpu.VMEM(blocks, jnp.bfloat16),
            pltpu.SemaphoreType.DMA((LAYERS, 1 + LAYERS)),
            pltpu.SemaphoreType.DMA((LAYERS,)),
        ),
        2,
        (0, 1),
        (0,),
    )(far(strip), far(screen))[0]


def forward(pieces, factor_real, factor_imag, second):
    blocks = shaped((ZX, SUB_ROWS * Y, LANES), jnp.bfloat16)
    phases = (2, LAYERS * PHASE_ROWS, LANES)
    twist_real, twist_imag = twiddle()
    return on_core(
        forward_kernel,
        "ahead",
        [blocks, blocks, pltpu.HBM(phases, jnp.float32)],
        (
            pltpu.VMEM(phases, jnp.float32),
            pltpu.VMEM((2, PHASE_ROWS, LANES), jnp.float32),
            pltpu.VMEM((2, SUB_ROWS * LINE_PITCH, LANES), jnp.float32),
            pltpu.SemaphoreType.DMA((LAYERS,)),
        ),
        7,
        far_out=(2,),
    )(pieces, twist_real, twist_imag, first_tables()[0], second, factor_real, factor_imag)


def backward(mine, other, phases, factor_real, factor_imag, second):
    twist_real, twist_imag = twiddle()
    return on_core(
        backward_kernel,
        "back",
        [shaped((LAYERS, 2, COLS, QUARTER), jnp.bfloat16)],
        (
            pltpu.VMEM((2, LAYERS * PHASE_ROWS, LANES), jnp.float32),
            pltpu.VMEM((2, STRIP_COLS * LINE_PITCH, LANES), jnp.float32),
            pltpu.VMEM((2, PHASE_ROWS, LANES), jnp.float32),
            pltpu.SemaphoreType.DMA((LAYERS,)),
        ),
        9,
        far_in=(2,),
    )(
        mine, other, far(phases), twist_real, twist_imag, first_tables()[1], second,
        factor_real, factor_imag,
    )[0]


def spread(cell_index, length, kernel_taps):
    tap_count = kernel_taps.shape[0]
    offset = (jnp.arange(length, dtype=jnp.int32)[None, :] - cell_index[:, None]) % length
    wanted = (jnp.arange(tap_count, dtype=jnp.int32) - tap_count // 2) % length
    matches = (offset[:, :, None] == wanted[None, None, :]).astype(jnp.float32)
    return jnp.sum(matches * kernel_taps, axis=2)


def prepare(row_cells, column_cells, plane, angle_table, kernel_taps):
    row_weights = spread(row_cells, SUB_ROWS, kernel_taps)
    column_weights = spread(column_cells, STRIP_COLS, kernel_taps)
    plane_pick = (plane[:, None] == jnp.arange(PLANES, dtype=jnp.int32)[None, :]).astype(
        jnp.float32
    )
    phase_angle = jnp.sum(plane_pick * angle_table[None, :], axis=1)
    return (row_weights, column_weights, jnp.cos(phase_angle), jnp.sin(phase_angle))


def degrid(subgrid, observed_vis, row_weights, column_weights, cosine, sine_part):
    kernel_rows = jnp.dot(row_weights, subgrid, precision=lax.Precision.HIGHEST)
    model_real = jnp.sum(kernel_rows[:, :STRIP_COLS] * column_weights, axis=1)
    model_imag = jnp.sum(kernel_rows[:, STRIP_COLS:] * column_weights, axis=1)
    residual_real = observed_vis[0] - (model_real * cosine - model_imag * sine_part)
    residual_imag = observed_vis[1] - (model_real * sine_part + model_imag * cosine)
    weighted_real = residual_real * cosine + residual_imag * sine_part
    weighted_imag = residual_imag * cosine - residual_real * sine_part
    spread_cols = jnp.concatenate(
        [weighted_real[:, None] * column_weights, weighted_imag[:, None] * column_weights], axis=1
    )
    adjoint = jnp.dot(row_weights.T, spread_cols, precision=lax.Precision.HIGHEST)
    return (jnp.stack([residual_real, residual_imag]), adjoint)


def exchange(blocks, axes, groups=None):
    return lax.all_to_all(
        blocks, axes, split_axis=0, concat_axis=0, tiled=True, axis_index_groups=groups
    )


def local(
    model_strip,
    screen_angle,
    facet_window,
    facet_shift,
    kernel_taps,
    plane_angle,
    u_cell,
    v_cell,
    w_plane,
    observed,
):
    swapped = lax.axis_index("facet") % CORE == 1

    pieces = exchange(gather(model_strip[0], screen_angle[0, 0]), "layer")

    factor_real, factor_imag = facet_factor(facet_window[0], facet_shift[0], swapped)
    plain = second_tables(STAGE_ORDER)
    crossed = second_tables(np.roll(STAGE_ORDER, SUBGRIDS // CORE))
    second_ahead = jnp.where(swapped, crossed[0], plain[0])
    second_back = jnp.where(swapped, crossed[1], plain[1])
    prepared = prepare(u_cell[0, 0], v_cell[0, 0], w_plane[0, 0], plane_angle[0], kernel_taps)
    observed_vis = (observed[0, 0, 0], observed[0, 0, 1])
    (
        pieces, factor_real, factor_imag, second_ahead, second_back, prepared, observed_vis
    ) = lax.optimization_barrier(
        (pieces, factor_real, factor_imag, second_ahead, second_back, prepared, observed_vis)
    )
    mine, other, phases = forward(pieces, factor_real, factor_imag, second_ahead)

    arrived = lax.ppermute(other, "facet", CORE_SWAP)
    pair_sum = (mine.astype(jnp.float32) + arrived.astype(jnp.float32)).astype(jnp.bfloat16)
    plane_terms = exchange(pair_sum, "facet", PLANE_GROUPS)
    table = pack_table()
    piece = (SUB_ROWS // 4, 2 * STRIP_COLS)
    packed = on_core(
        pack_kernel,
        "pack",
        [shaped((Y * LAYERS, *piece), jnp.bfloat16)],
        (pltpu.VMEM((SUB_ROWS * Y, LANES), jnp.float32),),
        2,
    )(plane_terms, table)[0]
    line_sum = jnp.sum(
        exchange(packed, ("layer", "facet"), LINE_GROUPS)
        .reshape(Y, LAYERS, *piece)
        .astype(jnp.float32),
        axis=0,
    )
    subgrid = (
        line_sum.reshape(LAYERS, SUB_ROWS // 4, 4, 2, COLS)
        .transpose(2, 1, 3, 0, 4)
        .reshape(SUB_ROWS, 2 * STRIP_COLS)
    )

    residual, adjoint = degrid(subgrid, observed_vis, *prepared)
    residual, adjoint = lax.optimization_barrier((residual, adjoint.astype(jnp.bfloat16)))

    sent = (
        adjoint.reshape(4, SUB_ROWS // 4, 2, LAYERS, COLS)
        .transpose(3, 1, 0, 2, 4)
        .reshape(1, LAYERS, *piece)
    )
    line = exchange(
        jnp.broadcast_to(sent, (Y, LAYERS, *piece)).reshape(Y * LAYERS, *piece),
        ("layer", "facet"),
        LINE_GROUPS,
    )
    copies = on_core(
        unpack_kernel,
        "unpack",
        [shaped((ZX, SUB_ROWS * Y, LANES), jnp.bfloat16)],
        (pltpu.VMEM((SUB_ROWS * Y, LANES), jnp.float32),),
        2,
    )(line, table)[0]
    mine_grids = exchange(copies, "facet", PLANE_GROUPS)
    other_grids = lax.ppermute(mine_grids, "facet", CORE_SWAP)
    leaving = backward(mine_grids, other_grids, phases, factor_real, factor_imag, second_back)
    gradient = (
        exchange(leaving, "layer")
        .transpose(1, 0, 2, 3)
        .reshape(1, 2, STRIP_COLS, QUARTER)
        .astype(jnp.float32)
    )
    return (residual[None, None], gradient)


def solution(mesh):
    return jax.shard_map(
        local,
        mesh=mesh,
        in_specs=(
            P("facet", None, None, "layer"),
            P("layer", "facet", None, None),
            P("facet", None),
            P("facet"),
            P(),
            P("layer", None),
            P("layer", "facet", None),
            P("layer", "facet", None),
            P("layer", "facet", None),
            P("layer", "facet", None, None),
        ),
        out_specs=(P("layer", "facet", None, None), P("facet", None, None, "layer")),
        check_vma=False,
    )
```

```python
import math

import jax
import jax.numpy as jnp
import numpy as np
from jax import lax
from jax.experimental import pallas as pl
from jax.experimental.pallas import tpu as pltpu
from jax.sharding import PartitionSpec as P

STRIP_LEN = 8192
SUB_ROWS = 64
STRIP_COLS = 64
PLANES = 8
SUBGRIDS = 128
LAYERS = 4
COLS = STRIP_COLS // LAYERS
QUARTER = STRIP_LEN // LAYERS
LANES = 128
BLOCKS = QUARTER // LANES

back_gain = 8.0

Y, Z, X, CORE = 8, 2, 4, 2
ZX = Z * X
FACET_INDEX = np.arange(SUBGRIDS).reshape(Y, Z, X, CORE)
STAGE_ORDER = FACET_INDEX.transpose(3, 1, 2, 0).reshape(-1)
PLANE_GROUPS = FACET_INDEX.transpose(0, 3, 1, 2).reshape(-1, ZX).tolist()
GLOBAL_INDEX = np.arange(LAYERS * SUBGRIDS).reshape(LAYERS, Y, Z, X, CORE)
LINE_GROUPS = GLOBAL_INDEX.transpose(2, 3, 4, 1, 0).reshape(-1, Y * LAYERS).tolist()
CORE_SWAP = [(i, i ^ 1) for i in range(SUBGRIDS)]

VMEM_LIMIT = 24 * 1024 * 1024

COL_PITCH = 24
LINE_PITCH = 72
PHASE_ROWS = SUB_ROWS * COL_PITCH


def even_series(function, degree):
    series = np.polynomial.chebyshev.Chebyshev.interpolate(
        lambda t: function(np.sqrt(np.maximum((t + 1.0) * 0.5, 0.0)) * math.pi), degree
    )
    return [float(value) for value in np.polynomial.chebyshev.cheb2poly(series.coef)]


COSINE_SERIES = even_series(np.cos, 6)
SINE_SERIES = even_series(lambda x: np.sinc(x / math.pi), 6)


def phase_parts(angle):
    t = angle * angle * (2.0 / (math.pi * math.pi)) - 1.0
    cosine = jnp.full_like(t, COSINE_SERIES[-1])
    sine = jnp.full_like(t, SINE_SERIES[-1])
    for value in COSINE_SERIES[-2::-1]:
        cosine = cosine * t + value
    for value in SINE_SERIES[-2::-1]:
        sine = sine * t + value
    return cosine, sine * angle


def fourier_table(rows, length):
    turn_count = rows[:, None] * np.arange(length)[None, :] % length
    angles = 2.0 * math.pi / length * turn_count
    table = np.stack([np.cos(angles), -np.sin(angles)]) / math.sqrt(length)
    return table.astype(np.float32).astype(jnp.bfloat16)


def twiddle():
    turn_count = np.arange(SUB_ROWS)[:, None] * np.arange(LANES)[None, :] % STRIP_LEN
    angles = 2.0 * math.pi / STRIP_LEN * turn_count
    return (np.cos(angles).astype(np.float32), (-np.sin(angles)).astype(np.float32))


def first_tables():
    real, imag = fourier_table(np.arange(SUB_ROWS), SUB_ROWS)
    ahead = np.block([[real, -imag], [imag, real]])
    back = np.block([[real.T, imag.T], [-imag.T, real.T]])
    return (ahead, back)


def second_tables(order):
    real, imag = fourier_table(order, SUBGRIDS)
    ahead = np.block([[real.T, imag.T], [-imag.T, real.T]])
    back = np.block([[real, -imag], [imag, real]])
    return (ahead, back)


def pack_table():
    table = np.zeros((4, 2, LAYERS, COLS, LAYERS, 4, 2, COLS), np.float32)
    for r in range(4):
        for p in range(2):
            for layer in range(LAYERS):
                for c in range(COLS):
                    table[r, p, layer, c, layer, r, p, c] = 1.0
    return table.reshape(4 * LANES, 4 * LANES).astype(jnp.bfloat16)


def facet_factor(window, shift_cells, swapped):
    def staged(values):
        ordered = values.reshape(Y, Z, X, CORE, SUB_ROWS).transpose(4, 3, 1, 2, 0)
        mine = ordered.reshape(SUB_ROWS, CORE, SUBGRIDS // CORE)
        return jnp.where(swapped, mine[:, ::-1], mine).reshape(SUB_ROWS, SUBGRIDS)

    positions = jnp.arange(STRIP_LEN, dtype=jnp.int32)
    turn_count = positions * shift_cells % STRIP_LEN
    angles = 2.0 * math.pi / STRIP_LEN * turn_count.astype(jnp.float32)
    return (staged(window * jnp.cos(angles)), staged(-window * jnp.sin(angles)))


def gather_kernel(strip, screen, out_ref, blocks, in_sems, out_sems):
    def arrivals(cq):
        rows = pl.ds(cq * COLS, COLS)
        pairs = [(screen.at[rows, :], blocks.at[cq, :, pl.ds(0, STRIP_LEN)])]
        for part in range(2):
            lanes = pl.ds(STRIP_LEN + part * QUARTER, QUARTER)
            pairs.append((strip.at[part, rows, :], blocks.at[cq, :, lanes]))
        return [
            pltpu.make_async_copy(source, target, in_sems.at[cq, i])
            for i, (source, target) in enumerate(pairs)
        ]

    def departure(cq):
        return pltpu.make_async_copy(blocks.at[cq], out_ref.at[cq], out_sems.at[cq])

    for cq in range(LAYERS):
        for copy in arrivals(cq):
            copy.start()
    for cq in range(LAYERS):
        for copy in arrivals(cq):
            copy.wait()
        departure(cq).start()
    for cq in range(LAYERS):
        departure(cq).wait()


def valid_rows(phases, layer):
    padded = phases.reshape(2, LAYERS * SUB_ROWS, COL_PITCH, LANES)
    return padded.at[:, pl.ds(layer * SUB_ROWS, SUB_ROWS), pl.ds(0, COLS), :]


def layer_rows(phases, layer):
    return phases.at[:, pl.ds(layer * SUB_ROWS, SUB_ROWS)]


def forward_kernel(
    pieces, twist_real, twist_imag, first, second, factor_real, factor_imag,
    mine_ref, other_ref, phases_out, phases, strip, half, sems,
):
    table = first[...]

    def strip_block(t, carry):
        for nq in range(LAYERS):
            rows = pl.ds(pl.multiple_of((nq * BLOCKS + t) * COL_PITCH, 8), COLS)
            for part in range(2):
                start = STRIP_LEN + part * QUARTER + t * LANES
                lanes = pl.ds(pl.multiple_of(start, LANES), LANES)
                strip[part, rows, :] = pieces[nq, :, lanes].astype(jnp.float32)
        return carry

    lax.fori_loop(0, BLOCKS, strip_block, 0, unroll=2)
    for layer in range(LAYERS):

        def phase_block(t, carry, layer=layer):
            for nq in range(LAYERS):
                lanes = pl.ds(pl.multiple_of(nq * QUARTER + t * LANES, LANES), LANES)
                cosine, sine = phase_parts(pieces[layer, :, lanes].astype(jnp.float32))
                rows = pl.ds(
                    pl.multiple_of(layer * PHASE_ROWS + (nq * BLOCKS + t) * COL_PITCH, 8), COLS
                )
                phases[0, rows, :] = cosine
                phases[1, rows, :] = sine
            return carry

        lax.fori_loop(0, BLOCKS, phase_block, 0, unroll=4)
        pltpu.make_async_copy(
            valid_rows(phases, layer), layer_rows(phases_out, layer), sems.at[layer]
        ).start()

        def first_block(pair, carry, layer=layer):
            c = pair * 2
            data = []
            for h in range(2):
                column = pl.ds(c + h, SUB_ROWS, stride=COL_PITCH)
                turn = pl.ds(layer * PHASE_ROWS + c + h, SUB_ROWS, stride=COL_PITCH)
                real, imag = strip[0, column, :], strip[1, column, :]
                cosine, sine = phases[0, turn, :], phases[1, turn, :]
                data.append(
                    jnp.concatenate(
                        [real * cosine - imag * sine, real * sine + imag * cosine], axis=0
                    )
                )
            data = jnp.concatenate(data, axis=1).astype(jnp.bfloat16)
            mixed = jnp.dot(table, data, preferred_element_type=jnp.float32)
            for h in range(2):
                real = mixed[:SUB_ROWS, h * LANES : (h + 1) * LANES]
                imag = mixed[SUB_ROWS:, h * LANES : (h + 1) * LANES]
                rows = pl.ds(layer * COLS + c + h, SUB_ROWS, stride=LINE_PITCH)
                half[0, rows, :] = real * twist_real[...] - imag * twist_imag[...]
                half[1, rows, :] = real * twist_imag[...] + imag * twist_real[...]
            return carry

        lax.fori_loop(0, COLS // 2, first_block, 0, unroll=8)

    weights = second[...]

    def second_block(pair, carry):
        data = []
        for h in range(2):
            rows = pl.ds(pl.multiple_of((pair * 2 + h) * LINE_PITCH, 8), STRIP_COLS)
            data.append(jnp.concatenate([half[0, rows, :], half[1, rows, :]], axis=1))
        data = jnp.concatenate(data, axis=0).astype(jnp.bfloat16)
        spectrum = jnp.dot(data, weights, preferred_element_type=jnp.float32)
        blocks = []
        for h in range(2):
            real = spectrum[h * STRIP_COLS : (h + 1) * STRIP_COLS, :LANES]
            imag = spectrum[h * STRIP_COLS : (h + 1) * STRIP_COLS, LANES:]
            fr = factor_real[pl.ds(pair * 2 + h, 1), :]
            fi = factor_imag[pl.ds(pair * 2 + h, 1), :]
            turned = jnp.concatenate([real * fr - imag * fi, real * fi + imag * fr], axis=0).T
            blocks.append(turned.reshape(CORE * ZX, Y, LANES))
        both = jnp.concatenate(blocks, axis=1).astype(jnp.bfloat16)
        place = pl.ds(pl.multiple_of(pair * 2 * Y, 2 * Y), 2 * Y)
        mine_ref[:, place, :] = both[:ZX]
        other_ref[:, place, :] = both[ZX:]
        return carry

    lax.fori_loop(0, SUB_ROWS // 2, second_block, 0, unroll=16)
    for layer in range(LAYERS):
        pltpu.make_async_copy(
            valid_rows(phases, layer), layer_rows(phases_out, layer), sems.at[layer]
        ).wait()


def pack_kernel(pieces, table, out_ref, total):
    total[...] = jnp.sum(pieces[...].astype(jnp.float32), axis=0)
    rows = []
    for y in range(Y):
        block = total[pl.ds(y, SUB_ROWS, stride=Y), :]
        rows.append(jnp.concatenate([block[r * 16 : (r + 1) * 16] for r in range(4)], axis=1))
    data = jnp.concatenate(rows, axis=0).astype(jnp.bfloat16)
    packed = jnp.dot(data, table[...], preferred_element_type=jnp.float32).astype(jnp.bfloat16)
    for y in range(Y):
        for layer in range(LAYERS):
            out_ref[y * LAYERS + layer] = packed[
                y * 16 : (y + 1) * 16, layer * LANES : (layer + 1) * LANES
            ]


def unpack_kernel(line, table, out_ref, total):
    data = jnp.concatenate(
        [
            jnp.concatenate([line[y * LAYERS + layer] for layer in range(LAYERS)], axis=1)
            for y in range(Y)
        ],
        axis=0,
    )
    grids = lax.dot_general(
        data, table[...], (((1,), (1,)), ((), ())), preferred_element_type=jnp.float32
    )
    for y in range(Y):
        for r in range(4):
            total[pl.ds(r * 16 * Y + y, 16, stride=Y), :] = grids[
                y * 16 : (y + 1) * 16, r * LANES : (r + 1) * LANES
            ]
    block = total[...].astype(jnp.bfloat16)
    for copy in range(ZX):
        out_ref[copy] = block


def backward_kernel(
    mine, other, phases_in, twist_real, twist_imag, first, second, factor_real, factor_imag,
    out_ref, phases, half, total, sems,
):
    for layer in range(LAYERS):
        pltpu.make_async_copy(
            layer_rows(phases_in, layer), valid_rows(phases, layer), sems.at[layer]
        ).start()
    weights = second[...]

    def second_block(pair, carry):
        place = pl.ds(pl.multiple_of(pair * 2 * Y, 2 * Y), 2 * Y)
        both = jnp.concatenate([mine[:, place, :], other[:, place, :]], axis=0).astype(jnp.float32)
        data = []
        for h in range(2):
            turned = both[:, h * Y : (h + 1) * Y, :].reshape(SUBGRIDS, LANES).T
            real = turned[:STRIP_COLS]
            imag = turned[STRIP_COLS:]
            fr = factor_real[pl.ds(pair * 2 + h, 1), :]
            fi = factor_imag[pl.ds(pair * 2 + h, 1), :]
            data.append(
                jnp.concatenate([real * fr + imag * fi, imag * fr - real * fi], axis=1)
            )
        data = jnp.concatenate(data, axis=0).astype(jnp.bfloat16)
        mixed = jnp.dot(data, weights, preferred_element_type=jnp.float32)
        for h in range(2):
            real = mixed[h * STRIP_COLS : (h + 1) * STRIP_COLS, :LANES]
            imag = mixed[h * STRIP_COLS : (h + 1) * STRIP_COLS, LANES:]
            tr = twist_real[pl.ds(pair * 2 + h, 1), :]
            ti = twist_imag[pl.ds(pair * 2 + h, 1), :]
            rows = pl.ds(pair * 2 + h, STRIP_COLS, stride=LINE_PITCH)
            half[0, rows, :] = real * tr + imag * ti
            half[1, rows, :] = imag * tr - real * ti
        return carry

    lax.fori_loop(0, SUB_ROWS // 2, second_block, 0, unroll=16)

    for layer in range(LAYERS):
        pltpu.make_async_copy(
            layer_rows(phases_in, layer), valid_rows(phases, layer), sems.at[layer]
        ).wait()
    table = first[...]

    def first_block(pair, carry):
        c = pair * 2
        sums = [None] * 4
        for j in range(LAYERS):

            def column(part, h, j=j):
                start = (j * COLS + c + h) * LINE_PITCH
                return half[part, pl.ds(pl.multiple_of(start, 8), SUB_ROWS), :]

            data = jnp.concatenate(
                [
                    jnp.concatenate([column(0, 0), column(1, 0)], axis=0),
                    jnp.concatenate([column(0, 1), column(1, 1)], axis=0),
                ],
                axis=1,
            ).astype(jnp.bfloat16)
            image = jnp.dot(table, data, preferred_element_type=jnp.float32)
            for h in range(2):
                real = image[:SUB_ROWS, h * LANES : (h + 1) * LANES]
                imag = image[SUB_ROWS:, h * LANES : (h + 1) * LANES]
                rows = pl.ds(j * PHASE_ROWS + c + h, SUB_ROWS, stride=COL_PITCH)
                cosine = phases[0, rows, :]
                sine = phases[1, rows, :]
                for part, term in enumerate(
                    (real * cosine + imag * sine, imag * cosine - real * sine)
                ):
                    place = 2 * h + part
                    sums[place] = term if j == 0 else sums[place] + term
        for h in range(2):
            for part in range(2):
                total[part, pl.ds(c + h, SUB_ROWS, stride=COL_PITCH), :] = back_gain * sums[2 * h + part]
        return carry

    lax.fori_loop(0, COLS // 2, first_block, 0, unroll=8)

    def leave_block(t, carry):
        lanes = pl.ds(pl.multiple_of(t * LANES, LANES), LANES)
        for nq in range(LAYERS):
            rows = pl.ds(pl.multiple_of((nq * BLOCKS + t) * COL_PITCH, 8), COLS)
            for part in range(2):
                out_ref[nq, part, :, lanes] = total[part, rows, :].astype(jnp.bfloat16)
        return carry

    lax.fori_loop(0, BLOCKS, leave_block, 0, unroll=2)


def join_kernel(terms, out_ref, total, sems):
    def departure(cq):
        rows = pl.ds(cq * COLS, COLS)
        return pltpu.make_async_copy(total.at[cq], out_ref.at[:, rows, :], sems.at[cq])

    for cq in range(LAYERS):
        total[cq] = terms[cq].astype(jnp.float32)
        departure(cq).start()
    for cq in range(LAYERS):
        departure(cq).wait()


def on_core(kernel, name, out_shape, scratch, inputs, far_in=(), far_out=()):
    near, far = pl.BlockSpec(memory_space=pltpu.VMEM), pl.BlockSpec(memory_space=pltpu.HBM)
    return pl.pallas_call(
        kernel,
        name=name,
        out_shape=out_shape,
        in_specs=[far if i in far_in else near for i in range(inputs)],
        out_specs=[far if i in far_out else near for i in range(len(out_shape))],
        scratch_shapes=list(scratch),
        compiler_params=pltpu.CompilerParams(vmem_limit_bytes=VMEM_LIMIT),
    )


def shaped(shape, kind):
    return jax.ShapeDtypeStruct(shape, kind)


def far(values):
    return pltpu.with_memory_space_constraint(values, pltpu.HBM)


def gather(strip, screen):
    blocks = (LAYERS, COLS, STRIP_LEN + 2 * QUARTER)
    return on_core(
        gather_kernel,
        "gather",
        [pltpu.HBM(blocks, jnp.bfloat16)],
        (
            pltpu.VMEM(blocks, jnp.bfloat16),
            pltpu.SemaphoreType.DMA((LAYERS, 3)),
            pltpu.SemaphoreType.DMA((LAYERS,)),
        ),
        2,
        (0, 1),
        (0,),
    )(far(strip), far(screen))[0]


def forward(pieces, factor_real, factor_imag, second):
    blocks = shaped((ZX, SUB_ROWS * Y, LANES), jnp.bfloat16)
    phases = (2, LAYERS * SUB_ROWS, COLS, LANES)
    twist_real, twist_imag = twiddle()
    return on_core(
        forward_kernel,
        "ahead",
        [blocks, blocks, pltpu.HBM(phases, jnp.float32)],
        (
            pltpu.VMEM((2, LAYERS * PHASE_ROWS, LANES), jnp.float32),
            pltpu.VMEM((2, PHASE_ROWS, LANES), jnp.float32),
            pltpu.VMEM((2, SUB_ROWS * LINE_PITCH, LANES), jnp.float32),
            pltpu.SemaphoreType.DMA((LAYERS,)),
        ),
        7,
        far_out=(2,),
    )(pieces, twist_real, twist_imag, first_tables()[0], second, factor_real, factor_imag)


def backward(mine, other, phases, factor_real, factor_imag, second):
    twist_real, twist_imag = twiddle()
    return on_core(
        backward_kernel,
        "back",
        [shaped((LAYERS, 2, COLS, QUARTER), jnp.bfloat16)],
        (
            pltpu.VMEM((2, LAYERS * PHASE_ROWS, LANES), jnp.float32),
            pltpu.VMEM((2, STRIP_COLS * LINE_PITCH, LANES), jnp.float32),
            pltpu.VMEM((2, PHASE_ROWS, LANES), jnp.float32),
            pltpu.SemaphoreType.DMA((LAYERS,)),
        ),
        9,
        far_in=(2,),
    )(
        mine, other, far(phases), twist_real, twist_imag, first_tables()[1], second,
        factor_real, factor_imag,
    )[0]


def spread(cell_index, length, kernel_taps):
    tap_count = kernel_taps.shape[0]
    offset = (jnp.arange(length, dtype=jnp.int32)[None, :] - cell_index[:, None]) % length
    wanted = (jnp.arange(tap_count, dtype=jnp.int32) - tap_count // 2) % length
    matches = (offset[:, :, None] == wanted[None, None, :]).astype(jnp.float32)
    return jnp.sum(matches * kernel_taps, axis=2)


def prepare(row_cells, column_cells, plane, angle_table, kernel_taps):
    row_weights = spread(row_cells, SUB_ROWS, kernel_taps)
    column_weights = spread(column_cells, STRIP_COLS, kernel_taps)
    plane_pick = (plane[:, None] == jnp.arange(PLANES, dtype=jnp.int32)[None, :]).astype(
        jnp.float32
    )
    phase_angle = jnp.sum(plane_pick * angle_table[None, :], axis=1)
    return (row_weights, column_weights, jnp.cos(phase_angle), jnp.sin(phase_angle))


def degrid(subgrid, observed_vis, row_weights, column_weights, cosine, sine_part):
    kernel_rows = jnp.dot(row_weights, subgrid, precision=lax.Precision.HIGHEST)
    model_real = jnp.sum(kernel_rows[:, :STRIP_COLS] * column_weights, axis=1)
    model_imag = jnp.sum(kernel_rows[:, STRIP_COLS:] * column_weights, axis=1)
    residual_real = observed_vis[0] - (model_real * cosine - model_imag * sine_part)
    residual_imag = observed_vis[1] - (model_real * sine_part + model_imag * cosine)
    weighted_real = residual_real * cosine + residual_imag * sine_part
    weighted_imag = residual_imag * cosine - residual_real * sine_part
    spread_cols = jnp.concatenate(
        [weighted_real[:, None] * column_weights, weighted_imag[:, None] * column_weights], axis=1
    )
    adjoint = jnp.dot(row_weights.T, spread_cols, precision=lax.Precision.HIGHEST)
    return ((residual_real, residual_imag), adjoint)


def exchange(blocks, axes, groups=None):
    return lax.all_to_all(
        blocks, axes, split_axis=0, concat_axis=0, tiled=True, axis_index_groups=groups
    )


def local(
    model_strip,
    screen_angle,
    facet_window,
    facet_shift,
    kernel_taps,
    plane_angle,
    u_cell,
    v_cell,
    w_plane,
    observed,
):
    swapped = lax.axis_index("facet") % CORE == 1

    pieces = exchange(gather(model_strip[0], screen_angle[0, 0]), "layer")

    factor_real, factor_imag = facet_factor(facet_window[0], facet_shift[0], swapped)
    plain = second_tables(STAGE_ORDER)
    crossed = second_tables(np.roll(STAGE_ORDER, SUBGRIDS // CORE))
    second_ahead = jnp.where(swapped, crossed[0], plain[0])
    second_back = jnp.where(swapped, crossed[1], plain[1])
    prepared = prepare(u_cell[0, 0], v_cell[0, 0], w_plane[0, 0], plane_angle[0], kernel_taps)
    observed_vis = (observed[0, 0, 0], observed[0, 0, 1])
    (
        pieces, factor_real, factor_imag, second_ahead, second_back, prepared, observed_vis
    ) = lax.optimization_barrier(
        (pieces, factor_real, factor_imag, second_ahead, second_back, prepared, observed_vis)
    )
    mine, other, phases = forward(pieces, factor_real, factor_imag, second_ahead)

    arrived = lax.ppermute(other, "facet", CORE_SWAP)
    pair_sum = (mine.astype(jnp.float32) + arrived.astype(jnp.float32)).astype(jnp.bfloat16)
    plane_terms = exchange(pair_sum, "facet", PLANE_GROUPS)
    table = pack_table()
    piece = (SUB_ROWS // 4, 2 * STRIP_COLS)
    packed = on_core(
        pack_kernel,
        "pack",
        [shaped((Y * LAYERS, *piece), jnp.bfloat16)],
        (pltpu.VMEM((SUB_ROWS * Y, LANES), jnp.float32),),
        2,
    )(plane_terms, table)[0]
    line_sum = jnp.sum(
        exchange(packed, ("layer", "facet"), LINE_GROUPS)
        .reshape(Y, LAYERS, *piece)
        .astype(jnp.float32),
        axis=0,
    )
    subgrid = (
        line_sum.reshape(LAYERS, SUB_ROWS // 4, 4, 2, COLS)
        .transpose(2, 1, 3, 0, 4)
        .reshape(SUB_ROWS, 2 * STRIP_COLS)
    )

    residual, adjoint = degrid(subgrid, observed_vis, *prepared)
    residual, adjoint = lax.optimization_barrier((residual, adjoint.astype(jnp.bfloat16)))

    sent = (
        adjoint.reshape(4, SUB_ROWS // 4, 2, LAYERS, COLS)
        .transpose(3, 1, 0, 2, 4)
        .reshape(1, LAYERS, *piece)
    )
    line = exchange(
        jnp.broadcast_to(sent, (Y, LAYERS, *piece)).reshape(Y * LAYERS, *piece),
        ("layer", "facet"),
        LINE_GROUPS,
    )
    copies = on_core(
        unpack_kernel,
        "unpack",
        [shaped((ZX, SUB_ROWS * Y, LANES), jnp.bfloat16)],
        (pltpu.VMEM((SUB_ROWS * Y, LANES), jnp.float32),),
        2,
    )(line, table)[0]
    mine_grids = exchange(copies, "facet", PLANE_GROUPS)
    mine_grids, residual = lax.optimization_barrier((mine_grids, residual))
    other_grids = lax.ppermute(mine_grids, "facet", CORE_SWAP)
    other_grids, residual = lax.optimization_barrier((other_grids, jnp.stack(residual)))
    leaving = backward(mine_grids, other_grids, phases, factor_real, factor_imag, second_back)
    gradient = on_core(
        join_kernel,
        "join",
        [pltpu.HBM((2, STRIP_COLS, QUARTER), jnp.float32)],
        (
            pltpu.VMEM((LAYERS, 2, COLS, QUARTER), jnp.float32),
            pltpu.SemaphoreType.DMA((LAYERS,)),
        ),
        1,
        far_out=(0,),
    )(exchange(leaving, "layer"))[0]
    return (residual[None, None], gradient[None])


def solution(mesh):
    return jax.shard_map(
        local,
        mesh=mesh,
        in_specs=(
            P("facet", None, None, "layer"),
            P("layer", "facet", None, None),
            P("facet", None),
            P("facet"),
            P(),
            P("layer", None),
            P("layer", "facet", None),
            P("layer", "facet", None),
            P("layer", "facet", None),
            P("layer", "facet", None, None),
        ),
        out_specs=(P("layer", "facet", None, None), P("facet", None, None, "layer")),
        check_vma=False,
    )
```

```python
import math

import jax
import jax.numpy as jnp
import numpy as np
from jax import lax
from jax.experimental import pallas as pl
from jax.experimental.pallas import tpu as pltpu
from jax.sharding import PartitionSpec as P

STRIP_LEN = 8192
SUB_ROWS = 64
STRIP_COLS = 64
PLANES = 8
SUBGRIDS = 128
LAYERS = 4
COLS = STRIP_COLS // LAYERS
QUARTER = STRIP_LEN // LAYERS
LANES = 128
BLOCKS = QUARTER // LANES

back_gain = 8.0

Y, Z, X, CORE = 8, 2, 4, 2
ZX = Z * X
FACET_INDEX = np.arange(SUBGRIDS).reshape(Y, Z, X, CORE)
STAGE_ORDER = FACET_INDEX.transpose(3, 1, 2, 0).reshape(-1)
PLANE_GROUPS = FACET_INDEX.transpose(0, 3, 1, 2).reshape(-1, ZX).tolist()
GLOBAL_INDEX = np.arange(LAYERS * SUBGRIDS).reshape(LAYERS, Y, Z, X, CORE)
LINE_GROUPS = GLOBAL_INDEX.transpose(2, 3, 4, 1, 0).reshape(-1, Y * LAYERS).tolist()
CORE_SWAP = [(i, i ^ 1) for i in range(SUBGRIDS)]

VMEM_LIMIT = 24 * 1024 * 1024

COL_PITCH = 24
LINE_PITCH = 72
PHASE_ROWS = SUB_ROWS * COL_PITCH


def even_series(function, degree):
    series = np.polynomial.chebyshev.Chebyshev.interpolate(
        lambda t: function(np.sqrt(np.maximum((t + 1.0) * 0.5, 0.0)) * math.pi), degree
    )
    return [float(value) for value in np.polynomial.chebyshev.cheb2poly(series.coef)]


COSINE_SERIES = even_series(np.cos, 6)
SINE_SERIES = even_series(lambda x: np.sinc(x / math.pi), 6)


def phase_parts(angle):
    t = angle * angle * (2.0 / (math.pi * math.pi)) - 1.0
    cosine = jnp.full_like(t, COSINE_SERIES[-1])
    sine = jnp.full_like(t, SINE_SERIES[-1])
    for value in COSINE_SERIES[-2::-1]:
        cosine = cosine * t + value
    for value in SINE_SERIES[-2::-1]:
        sine = sine * t + value
    return cosine, sine * angle


def fourier_table(rows, length):
    turn_count = rows[:, None] * np.arange(length)[None, :] % length
    angles = 2.0 * math.pi / length * turn_count
    table = np.stack([np.cos(angles), -np.sin(angles)]) / math.sqrt(length)
    return table.astype(np.float32).astype(jnp.bfloat16)


def twiddle():
    turn_count = np.arange(SUB_ROWS)[:, None] * np.arange(LANES)[None, :] % STRIP_LEN
    angles = 2.0 * math.pi / STRIP_LEN * turn_count
    return (np.cos(angles).astype(np.float32), (-np.sin(angles)).astype(np.float32))


def first_tables():
    real, imag = fourier_table(np.arange(SUB_ROWS), SUB_ROWS)
    ahead = np.block([[real, -imag], [imag, real]])
    back = np.block([[real.T, imag.T], [-imag.T, real.T]])
    return (ahead, back)


def second_tables(order):
    real, imag = fourier_table(order, SUBGRIDS)
    ahead = np.block([[real.T, imag.T], [-imag.T, real.T]])
    back = np.block([[real, -imag], [imag, real]])
    return (ahead, back)


def pack_table():
    table = np.zeros((4, 2, LAYERS, COLS, LAYERS, 4, 2, COLS), np.float32)
    for r in range(4):
        for p in range(2):
            for layer in range(LAYERS):
                for c in range(COLS):
                    table[r, p, layer, c, layer, r, p, c] = 1.0
    return table.reshape(4 * LANES, 4 * LANES).astype(jnp.bfloat16)


def facet_factor(window, shift_cells, swapped):
    def staged(values):
        ordered = values.reshape(Y, Z, X, CORE, SUB_ROWS).transpose(4, 3, 1, 2, 0)
        mine = ordered.reshape(SUB_ROWS, CORE, SUBGRIDS // CORE)
        return jnp.where(swapped, mine[:, ::-1], mine).reshape(SUB_ROWS, SUBGRIDS)

    positions = jnp.arange(STRIP_LEN, dtype=jnp.int32)
    turn_count = positions * shift_cells % STRIP_LEN
    angles = 2.0 * math.pi / STRIP_LEN * turn_count.astype(jnp.float32)
    return (staged(window * jnp.cos(angles)), staged(-window * jnp.sin(angles)))


def gather_kernel(strip, screen, out_ref, blocks, in_sems, out_sems):
    def arrivals(cq):
        rows = pl.ds(cq * COLS, COLS)
        pairs = [(screen.at[rows, :], blocks.at[cq, :, pl.ds(0, STRIP_LEN)])]
        for part in range(2):
            lanes = pl.ds(STRIP_LEN + part * QUARTER, QUARTER)
            pairs.append((strip.at[part, rows, :], blocks.at[cq, :, lanes]))
        return [
            pltpu.make_async_copy(source, target, in_sems.at[cq, i])
            for i, (source, target) in enumerate(pairs)
        ]

    def departure(cq):
        return pltpu.make_async_copy(blocks.at[cq], out_ref.at[cq], out_sems.at[cq])

    for cq in range(LAYERS):
        for copy in arrivals(cq):
            copy.start()
    for cq in range(LAYERS):
        for copy in arrivals(cq):
            copy.wait()
        departure(cq).start()
    for cq in range(LAYERS):
        departure(cq).wait()


def valid_rows(phases, layer):
    padded = phases.reshape(2, LAYERS * SUB_ROWS + 1, COL_PITCH, LANES)
    return padded.at[:, pl.ds(layer * SUB_ROWS, SUB_ROWS), pl.ds(0, COLS), :]


def layer_rows(phases, layer):
    return phases.at[:, pl.ds(layer * SUB_ROWS, SUB_ROWS)]


def forward_kernel(
    pieces, twist_real, twist_imag, first, second, factor_real, factor_imag,
    mine_ref, other_ref, phases_out, phases, strip, half, sems,
):
    table = first[...]

    def strip_block(t, carry):
        for nq in range(LAYERS):
            rows = pl.ds(pl.multiple_of((nq * BLOCKS + t) * COL_PITCH, 8), COLS)
            for part in range(2):
                start = STRIP_LEN + part * QUARTER + t * LANES
                lanes = pl.ds(pl.multiple_of(start, LANES), LANES)
                strip[part, rows, :] = pieces[nq, :, lanes].astype(jnp.float32)
        return carry

    lax.fori_loop(0, BLOCKS, strip_block, 0, unroll=4)
    for layer in range(LAYERS):

        def phase_block(t, carry, layer=layer):
            for nq in range(LAYERS):
                lanes = pl.ds(pl.multiple_of(nq * QUARTER + t * LANES, LANES), LANES)
                cosine, sine = phase_parts(pieces[layer, :, lanes].astype(jnp.float32))
                rows = pl.ds(
                    pl.multiple_of(layer * PHASE_ROWS + (nq * BLOCKS + t) * COL_PITCH, 8), COLS
                )
                phases[0, rows, :] = cosine
                phases[1, rows, :] = sine
            return carry

        lax.fori_loop(0, BLOCKS, phase_block, 0, unroll=8)
        pltpu.make_async_copy(
            valid_rows(phases, layer), layer_rows(phases_out, layer), sems.at[layer]
        ).start()

    def first_block(pair, carry):
        c = pair * 2
        columns = []
        for h in range(2):
            rows = pl.ds(c + h, SUB_ROWS, stride=COL_PITCH)
            columns.append((strip[0, rows, :], strip[1, rows, :]))
        for layer in range(LAYERS):
            data = []
            for h, (real, imag) in enumerate(columns):
                turn = pl.ds(layer * PHASE_ROWS + c + h, SUB_ROWS, stride=COL_PITCH)
                cosine, sine = phases[0, turn, :], phases[1, turn, :]
                data.append(
                    jnp.concatenate(
                        [real * cosine - imag * sine, real * sine + imag * cosine], axis=0
                    )
                )
            data = jnp.concatenate(data, axis=1).astype(jnp.bfloat16)
            mixed = jnp.dot(table, data, preferred_element_type=jnp.float32)
            for h in range(2):
                real = mixed[:SUB_ROWS, h * LANES : (h + 1) * LANES]
                imag = mixed[SUB_ROWS:, h * LANES : (h + 1) * LANES]
                rows = pl.ds(layer * COLS + c + h, SUB_ROWS, stride=LINE_PITCH)
                half[0, rows, :] = real * twist_real[...] - imag * twist_imag[...]
                half[1, rows, :] = real * twist_imag[...] + imag * twist_real[...]
        return carry

    lax.fori_loop(0, COLS // 2, first_block, 0, unroll=2)

    weights = second[...]

    def second_block(pair, carry):
        data = []
        for h in range(2):
            rows = pl.ds(pl.multiple_of((pair * 2 + h) * LINE_PITCH, 8), STRIP_COLS)
            data.append(jnp.concatenate([half[0, rows, :], half[1, rows, :]], axis=1))
        data = jnp.concatenate(data, axis=0).astype(jnp.bfloat16)
        spectrum = jnp.dot(data, weights, preferred_element_type=jnp.float32)
        blocks = []
        for h in range(2):
            real = spectrum[h * STRIP_COLS : (h + 1) * STRIP_COLS, :LANES]
            imag = spectrum[h * STRIP_COLS : (h + 1) * STRIP_COLS, LANES:]
            fr = factor_real[pl.ds(pair * 2 + h, 1), :]
            fi = factor_imag[pl.ds(pair * 2 + h, 1), :]
            turned = jnp.concatenate([real * fr - imag * fi, real * fi + imag * fr], axis=0).T
            blocks.append(turned.reshape(CORE * ZX, Y, LANES))
        both = jnp.concatenate(blocks, axis=1).astype(jnp.bfloat16)
        place = pl.ds(pl.multiple_of(pair * 2 * Y, 2 * Y), 2 * Y)
        mine_ref[:, place, :] = both[:ZX]
        other_ref[:, place, :] = both[ZX:]
        return carry

    lax.fori_loop(0, SUB_ROWS // 2, second_block, 0, unroll=16)
    for layer in range(LAYERS):
        pltpu.make_async_copy(
            valid_rows(phases, layer), layer_rows(phases_out, layer), sems.at[layer]
        ).wait()


def pack_kernel(pieces, table, out_ref, total):
    total[: SUB_ROWS * Y, :] = jnp.sum(pieces[...].astype(jnp.float32), axis=0)
    rows = []
    for y in range(Y):
        block = total[pl.ds(y, SUB_ROWS, stride=Y), :]
        rows.append(jnp.concatenate([block[r * 16 : (r + 1) * 16] for r in range(4)], axis=1))
    data = jnp.concatenate(rows, axis=0).astype(jnp.bfloat16)
    packed = jnp.dot(data, table[...], preferred_element_type=jnp.float32).astype(jnp.bfloat16)
    for y in range(Y):
        for layer in range(LAYERS):
            out_ref[y * LAYERS + layer] = packed[
                y * 16 : (y + 1) * 16, layer * LANES : (layer + 1) * LANES
            ]


def unpack_kernel(line, table, out_ref, total):
    data = jnp.concatenate(
        [
            jnp.concatenate([line[y * LAYERS + layer] for layer in range(LAYERS)], axis=1)
            for y in range(Y)
        ],
        axis=0,
    )
    grids = lax.dot_general(
        data, table[...], (((1,), (1,)), ((), ())), preferred_element_type=jnp.float32
    )
    for y in range(Y):
        for r in range(4):
            total[pl.ds(r * 16 * Y + y, 16, stride=Y), :] = grids[
                y * 16 : (y + 1) * 16, r * LANES : (r + 1) * LANES
            ]
    block = total[: SUB_ROWS * Y, :].astype(jnp.bfloat16)
    for copy in range(ZX):
        out_ref[copy] = block


def backward_kernel(
    mine, other, phases_in, twist_real, twist_imag, first, second, factor_real, factor_imag,
    out_ref, phases, half, total, sems,
):
    for layer in range(LAYERS):
        pltpu.make_async_copy(
            layer_rows(phases_in, layer), valid_rows(phases, layer), sems.at[layer]
        ).start()
    weights = second[...]

    def second_block(pair, carry):
        place = pl.ds(pl.multiple_of(pair * 2 * Y, 2 * Y), 2 * Y)
        both = jnp.concatenate([mine[:, place, :], other[:, place, :]], axis=0).astype(jnp.float32)
        data = []
        for h in range(2):
            turned = both[:, h * Y : (h + 1) * Y, :].reshape(SUBGRIDS, LANES).T
            real = turned[:STRIP_COLS]
            imag = turned[STRIP_COLS:]
            fr = factor_real[pl.ds(pair * 2 + h, 1), :]
            fi = factor_imag[pl.ds(pair * 2 + h, 1), :]
            data.append(
                jnp.concatenate([real * fr + imag * fi, imag * fr - real * fi], axis=1)
            )
        data = jnp.concatenate(data, axis=0).astype(jnp.bfloat16)
        mixed = jnp.dot(data, weights, preferred_element_type=jnp.float32)
        for h in range(2):
            real = mixed[h * STRIP_COLS : (h + 1) * STRIP_COLS, :LANES]
            imag = mixed[h * STRIP_COLS : (h + 1) * STRIP_COLS, LANES:]
            tr = twist_real[pl.ds(pair * 2 + h, 1), :]
            ti = twist_imag[pl.ds(pair * 2 + h, 1), :]
            rows = pl.ds(pair * 2 + h, STRIP_COLS, stride=LINE_PITCH)
            half[0, rows, :] = real * tr + imag * ti
            half[1, rows, :] = imag * tr - real * ti
        return carry

    lax.fori_loop(0, SUB_ROWS // 2, second_block, 0, unroll=16)

    for layer in range(LAYERS):
        pltpu.make_async_copy(
            layer_rows(phases_in, layer), valid_rows(phases, layer), sems.at[layer]
        ).wait()
    table = first[...]

    def first_block(pair, carry):
        c = pair * 2
        sums = [None] * 4
        for j in range(LAYERS):

            def column(part, h, j=j):
                start = (j * COLS + c + h) * LINE_PITCH
                return half[part, pl.ds(pl.multiple_of(start, 8), SUB_ROWS), :]

            data = jnp.concatenate(
                [
                    jnp.concatenate([column(0, 0), column(1, 0)], axis=0),
                    jnp.concatenate([column(0, 1), column(1, 1)], axis=0),
                ],
                axis=1,
            ).astype(jnp.bfloat16)
            image = jnp.dot(table, data, preferred_element_type=jnp.float32)
            for h in range(2):
                real = image[:SUB_ROWS, h * LANES : (h + 1) * LANES]
                imag = image[SUB_ROWS:, h * LANES : (h + 1) * LANES]
                rows = pl.ds(j * PHASE_ROWS + c + h, SUB_ROWS, stride=COL_PITCH)
                cosine = phases[0, rows, :]
                sine = phases[1, rows, :]
                for part, term in enumerate(
                    (real * cosine + imag * sine, imag * cosine - real * sine)
                ):
                    place = 2 * h + part
                    sums[place] = term if j == 0 else sums[place] + term
        for h in range(2):
            for part in range(2):
                total[part, pl.ds(c + h, SUB_ROWS, stride=COL_PITCH), :] = back_gain * sums[2 * h + part]
        return carry

    lax.fori_loop(0, COLS // 2, first_block, 0, unroll=8)

    def leave_block(t, carry):
        lanes = pl.ds(pl.multiple_of(t * LANES, LANES), LANES)
        for nq in range(LAYERS):
            rows = pl.ds(pl.multiple_of((nq * BLOCKS + t) * COL_PITCH, 8), COLS)
            for part in range(2):
                out_ref[nq, part, :, lanes] = total[part, rows, :].astype(jnp.bfloat16)
        return carry

    lax.fori_loop(0, BLOCKS, leave_block, 0, unroll=2)


def join_kernel(terms, out_ref, total, sems):
    def departure(cq):
        rows = pl.ds(cq * COLS, COLS)
        return pltpu.make_async_copy(total.at[cq], out_ref.at[:, rows, :], sems.at[cq])

    for cq in range(LAYERS):
        total[cq] = terms[cq].astype(jnp.float32)
        departure(cq).start()
    for cq in range(LAYERS):
        departure(cq).wait()


def on_core(kernel, name, out_shape, scratch, inputs, far_in=(), far_out=()):
    near, far = pl.BlockSpec(memory_space=pltpu.VMEM), pl.BlockSpec(memory_space=pltpu.HBM)
    return pl.pallas_call(
        kernel,
        name=name,
        out_shape=out_shape,
        in_specs=[far if i in far_in else near for i in range(inputs)],
        out_specs=[far if i in far_out else near for i in range(len(out_shape))],
        scratch_shapes=list(scratch),
        compiler_params=pltpu.CompilerParams(vmem_limit_bytes=VMEM_LIMIT),
    )


def shaped(shape, kind):
    return jax.ShapeDtypeStruct(shape, kind)


def far(values):
    return pltpu.with_memory_space_constraint(values, pltpu.HBM)


def gather(strip, screen):
    blocks = (LAYERS, COLS, STRIP_LEN + 2 * QUARTER)
    return on_core(
        gather_kernel,
        "gather",
        [pltpu.HBM(blocks, jnp.bfloat16)],
        (
            pltpu.VMEM(blocks, jnp.bfloat16),
            pltpu.SemaphoreType.DMA((LAYERS, 3)),
            pltpu.SemaphoreType.DMA((LAYERS,)),
        ),
        2,
        (0, 1),
        (0,),
    )(far(strip), far(screen))[0]


def forward(pieces, factor_real, factor_imag, second):
    blocks = shaped((ZX, SUB_ROWS * Y, LANES), jnp.bfloat16)
    phases = (2, LAYERS * SUB_ROWS, COLS, LANES)
    twist_real, twist_imag = twiddle()
    return on_core(
        forward_kernel,
        "ahead",
        [blocks, blocks, pltpu.HBM(phases, jnp.float32)],
        (
            pltpu.VMEM((2, LAYERS * PHASE_ROWS + COL_PITCH, LANES), jnp.float32),
            pltpu.VMEM((2, PHASE_ROWS + COL_PITCH, LANES), jnp.float32),
            pltpu.VMEM((2, (SUB_ROWS + 1) * LINE_PITCH, LANES), jnp.float32),
            pltpu.SemaphoreType.DMA((LAYERS,)),
        ),
        7,
        far_out=(2,),
    )(pieces, twist_real, twist_imag, first_tables()[0], second, factor_real, factor_imag)


def backward(mine, other, phases, factor_real, factor_imag, second):
    twist_real, twist_imag = twiddle()
    return on_core(
        backward_kernel,
        "back",
        [shaped((LAYERS, 2, COLS, QUARTER), jnp.bfloat16)],
        (
            pltpu.VMEM((2, LAYERS * PHASE_ROWS + COL_PITCH, LANES), jnp.float32),
            pltpu.VMEM((2, (STRIP_COLS + 1) * LINE_PITCH, LANES), jnp.float32),
            pltpu.VMEM((2, PHASE_ROWS + COL_PITCH, LANES), jnp.float32),
            pltpu.SemaphoreType.DMA((LAYERS,)),
        ),
        9,
        far_in=(2,),
    )(
        mine, other, far(phases), twist_real, twist_imag, first_tables()[1], second,
        factor_real, factor_imag,
    )[0]


def spread(cell_index, length, kernel_taps):
    tap_count = kernel_taps.shape[0]
    offset = (jnp.arange(length, dtype=jnp.int32)[None, :] - cell_index[:, None]) % length
    wanted = (jnp.arange(tap_count, dtype=jnp.int32) - tap_count // 2) % length
    matches = (offset[:, :, None] == wanted[None, None, :]).astype(jnp.float32)
    return jnp.sum(matches * kernel_taps, axis=2)


def prepare(row_cells, column_cells, plane, angle_table, kernel_taps):
    row_weights = spread(row_cells, SUB_ROWS, kernel_taps)
    column_weights = spread(column_cells, STRIP_COLS, kernel_taps)
    plane_pick = (plane[:, None] == jnp.arange(PLANES, dtype=jnp.int32)[None, :]).astype(
        jnp.float32
    )
    phase_angle = jnp.sum(plane_pick * angle_table[None, :], axis=1)
    return (row_weights, column_weights, jnp.cos(phase_angle), jnp.sin(phase_angle))


def degrid(subgrid, observed_vis, row_weights, column_weights, cosine, sine_part):
    kernel_rows = jnp.dot(row_weights, subgrid, precision=lax.Precision.HIGHEST)
    model_real = jnp.sum(kernel_rows[:, :STRIP_COLS] * column_weights, axis=1)
    model_imag = jnp.sum(kernel_rows[:, STRIP_COLS:] * column_weights, axis=1)
    residual_real = observed_vis[0] - (model_real * cosine - model_imag * sine_part)
    residual_imag = observed_vis[1] - (model_real * sine_part + model_imag * cosine)
    weighted_real = residual_real * cosine + residual_imag * sine_part
    weighted_imag = residual_imag * cosine - residual_real * sine_part
    spread_cols = jnp.concatenate(
        [weighted_real[:, None] * column_weights, weighted_imag[:, None] * column_weights], axis=1
    )
    adjoint = jnp.dot(row_weights.T, spread_cols, precision=lax.Precision.HIGHEST)
    return ((residual_real, residual_imag), adjoint)


def exchange(blocks, axes, groups=None):
    return lax.all_to_all(
        blocks, axes, split_axis=0, concat_axis=0, tiled=True, axis_index_groups=groups
    )


def local(
    model_strip,
    screen_angle,
    facet_window,
    facet_shift,
    kernel_taps,
    plane_angle,
    u_cell,
    v_cell,
    w_plane,
    observed,
):
    swapped = lax.axis_index("facet") % CORE == 1

    pieces = exchange(gather(model_strip[0], screen_angle[0, 0]), "layer")

    factor_real, factor_imag = facet_factor(facet_window[0], facet_shift[0], swapped)
    plain = second_tables(STAGE_ORDER)
    crossed = second_tables(np.roll(STAGE_ORDER, SUBGRIDS // CORE))
    second_ahead = jnp.where(swapped, crossed[0], plain[0])
    second_back = jnp.where(swapped, crossed[1], plain[1])
    prepared = prepare(u_cell[0, 0], v_cell[0, 0], w_plane[0, 0], plane_angle[0], kernel_taps)
    observed_vis = (observed[0, 0, 0], observed[0, 0, 1])
    (
        pieces, factor_real, factor_imag, second_ahead, second_back, prepared, observed_vis
    ) = lax.optimization_barrier(
        (pieces, factor_real, factor_imag, second_ahead, second_back, prepared, observed_vis)
    )
    mine, other, phases = forward(pieces, factor_real, factor_imag, second_ahead)

    arrived = lax.ppermute(other, "facet", CORE_SWAP)
    pair_sum = (mine.astype(jnp.float32) + arrived.astype(jnp.float32)).astype(jnp.bfloat16)
    plane_terms = exchange(pair_sum, "facet", PLANE_GROUPS)
    table = pack_table()
    piece = (SUB_ROWS // 4, 2 * STRIP_COLS)
    packed = on_core(
        pack_kernel,
        "pack",
        [shaped((Y * LAYERS, *piece), jnp.bfloat16)],
        (pltpu.VMEM((SUB_ROWS * Y + Y, LANES), jnp.float32),),
        2,
    )(plane_terms, table)[0]
    line_sum = jnp.sum(
        exchange(packed, ("layer", "facet"), LINE_GROUPS)
        .reshape(Y, LAYERS, *piece)
        .astype(jnp.float32),
        axis=0,
    )
    subgrid = (
        line_sum.reshape(LAYERS, SUB_ROWS // 4, 4, 2, COLS)
        .transpose(2, 1, 3, 0, 4)
        .reshape(SUB_ROWS, 2 * STRIP_COLS)
    )

    residual, adjoint = degrid(subgrid, observed_vis, *prepared)
    residual, adjoint = lax.optimization_barrier((residual, adjoint.astype(jnp.bfloat16)))

    sent = (
        adjoint.reshape(4, SUB_ROWS // 4, 2, LAYERS, COLS)
        .transpose(3, 1, 0, 2, 4)
        .reshape(1, LAYERS, *piece)
    )
    line = exchange(
        jnp.broadcast_to(sent, (Y, LAYERS, *piece)).reshape(Y * LAYERS, *piece),
        ("layer", "facet"),
        LINE_GROUPS,
    )
    copies = on_core(
        unpack_kernel,
        "unpack",
        [shaped((ZX, SUB_ROWS * Y, LANES), jnp.bfloat16)],
        (pltpu.VMEM((SUB_ROWS * Y + Y, LANES), jnp.float32),),
        2,
    )(line, table)[0]
    mine_grids = exchange(copies, "facet", PLANE_GROUPS)
    mine_grids, residual = lax.optimization_barrier((mine_grids, residual))
    other_grids = lax.ppermute(mine_grids, "facet", CORE_SWAP)
    other_grids, residual = lax.optimization_barrier((other_grids, jnp.stack(residual)))
    leaving = backward(mine_grids, other_grids, phases, factor_real, factor_imag, second_back)
    gradient = on_core(
        join_kernel,
        "join",
        [pltpu.HBM((2, STRIP_COLS, QUARTER), jnp.float32)],
        (
            pltpu.VMEM((LAYERS, 2, COLS, QUARTER), jnp.float32),
            pltpu.SemaphoreType.DMA((LAYERS,)),
        ),
        1,
        far_out=(0,),
    )(exchange(leaving, "layer"))[0]
    return (residual[None, None], gradient[None])


def solution(mesh):
    return jax.shard_map(
        local,
        mesh=mesh,
        in_specs=(
            P("facet", None, None, "layer"),
            P("layer", "facet", None, None),
            P("facet", None),
            P("facet"),
            P(),
            P("layer", None),
            P("layer", "facet", None),
            P("layer", "facet", None),
            P("layer", "facet", None),
            P("layer", "facet", None, None),
        ),
        out_specs=(P("layer", "facet", None, None), P("facet", None, None, "layer")),
        check_vma=False,
    )
```

```python
import math

import jax
import jax.numpy as jnp
import numpy as np
from jax import lax
from jax.experimental import pallas as pl
from jax.experimental.pallas import tpu as pltpu
from jax.sharding import PartitionSpec as P

STRIP_LEN = 8192
SUB_ROWS = 64
STRIP_COLS = 64
PLANES = 8
SUBGRIDS = 128
LAYERS = 4
COLS = STRIP_COLS // LAYERS
QUARTER = STRIP_LEN // LAYERS
LANES = 128
BLOCKS = QUARTER // LANES

back_gain = 8.0

Y, Z, X, CORE = 8, 2, 4, 2
ZX = Z * X
FACET_INDEX = np.arange(SUBGRIDS).reshape(Y, Z, X, CORE)
STAGE_ORDER = FACET_INDEX.transpose(3, 1, 2, 0).reshape(-1)
PLANE_GROUPS = FACET_INDEX.transpose(0, 3, 1, 2).reshape(-1, ZX).tolist()
GLOBAL_INDEX = np.arange(LAYERS * SUBGRIDS).reshape(LAYERS, Y, Z, X, CORE)
LINE_GROUPS = GLOBAL_INDEX.transpose(2, 3, 4, 1, 0).reshape(-1, Y * LAYERS).tolist()
CORE_SWAP = [(i, i ^ 1) for i in range(SUBGRIDS)]

VMEM_LIMIT = 24 * 1024 * 1024

COL_PITCH = 24
LINE_PITCH = 72
PHASE_ROWS = SUB_ROWS * COL_PITCH


def even_series(function, degree):
    series = np.polynomial.chebyshev.Chebyshev.interpolate(
        lambda t: function(np.sqrt(np.maximum((t + 1.0) * 0.5, 0.0)) * math.pi), degree
    )
    return [float(value) for value in np.polynomial.chebyshev.cheb2poly(series.coef)]


COSINE_SERIES = even_series(np.cos, 6)
SINE_SERIES = even_series(lambda x: np.sinc(x / math.pi), 6)


def phase_parts(angle):
    t = angle * angle * (2.0 / (math.pi * math.pi)) - 1.0
    cosine = jnp.full_like(t, COSINE_SERIES[-1])
    sine = jnp.full_like(t, SINE_SERIES[-1])
    for value in COSINE_SERIES[-2::-1]:
        cosine = cosine * t + value
    for value in SINE_SERIES[-2::-1]:
        sine = sine * t + value
    return cosine, sine * angle


def fourier_table(rows, length):
    turn_count = rows[:, None] * np.arange(length)[None, :] % length
    angles = 2.0 * math.pi / length * turn_count
    table = np.stack([np.cos(angles), -np.sin(angles)]) / math.sqrt(length)
    return table.astype(np.float32).astype(jnp.bfloat16)


def twiddle():
    turn_count = np.arange(SUB_ROWS)[:, None] * np.arange(LANES)[None, :] % STRIP_LEN
    angles = 2.0 * math.pi / STRIP_LEN * turn_count
    return (np.cos(angles).astype(np.float32), (-np.sin(angles)).astype(np.float32))


def first_tables():
    real, imag = fourier_table(np.arange(SUB_ROWS), SUB_ROWS)
    ahead = np.block([[real, -imag], [imag, real]])
    back = np.block([[real.T, imag.T], [-imag.T, real.T]])
    return (ahead, back)


def second_tables(order):
    real, imag = fourier_table(order, SUBGRIDS)
    ahead = np.block([[real.T, imag.T], [-imag.T, real.T]])
    back = np.block([[real, -imag], [imag, real]])
    return (ahead, back)


def pack_table():
    table = np.zeros((4, 2, LAYERS, COLS, LAYERS, 4, 2, COLS), np.float32)
    for r in range(4):
        for p in range(2):
            for layer in range(LAYERS):
                for c in range(COLS):
                    table[r, p, layer, c, layer, r, p, c] = 1.0
    return table.reshape(4 * LANES, 4 * LANES).astype(jnp.bfloat16)


def facet_factor(window, shift_cells, swapped):
    def staged(values):
        ordered = values.reshape(Y, Z, X, CORE, SUB_ROWS).transpose(4, 3, 1, 2, 0)
        mine = ordered.reshape(SUB_ROWS, CORE, SUBGRIDS // CORE)
        return jnp.where(swapped, mine[:, ::-1], mine).reshape(SUB_ROWS, SUBGRIDS)

    positions = jnp.arange(STRIP_LEN, dtype=jnp.int32)
    turn_count = positions * shift_cells % STRIP_LEN
    angles = 2.0 * math.pi / STRIP_LEN * turn_count.astype(jnp.float32)
    return (staged(window * jnp.cos(angles)), staged(-window * jnp.sin(angles)))


def gather_kernel(strip, screen, out_ref, blocks, in_sems, out_sems):
    def arrivals(cq):
        rows = pl.ds(cq * COLS, COLS)
        pairs = [(screen.at[rows, :], blocks.at[cq, :, pl.ds(0, STRIP_LEN)])]
        for part in range(2):
            lanes = pl.ds(STRIP_LEN + part * QUARTER, QUARTER)
            pairs.append((strip.at[part, rows, :], blocks.at[cq, :, lanes]))
        return [
            pltpu.make_async_copy(source, target, in_sems.at[cq, i])
            for i, (source, target) in enumerate(pairs)
        ]

    def departure(cq):
        return pltpu.make_async_copy(blocks.at[cq], out_ref.at[cq], out_sems.at[cq])

    for cq in range(LAYERS):
        for copy in arrivals(cq):
            copy.start()
    for cq in range(LAYERS):
        for copy in arrivals(cq):
            copy.wait()
        departure(cq).start()
    for cq in range(LAYERS):
        departure(cq).wait()


def valid_rows(phases, layer):
    padded = phases.reshape(2, LAYERS * SUB_ROWS + 1, COL_PITCH, LANES)
    return padded.at[:, pl.ds(layer * SUB_ROWS, SUB_ROWS), pl.ds(0, COLS), :]


def layer_rows(phases, layer):
    return phases.at[:, pl.ds(layer * SUB_ROWS, SUB_ROWS)]


def forward_kernel(
    pieces, twist_real, twist_imag, first, second, factor_real, factor_imag,
    mine_ref, other_ref, phases_out, phases, strip, half, sems,
):
    table = first[...]

    def strip_block(t, carry):
        for nq in range(LAYERS):
            rows = pl.ds(pl.multiple_of((nq * BLOCKS + t) * COL_PITCH, 8), COLS)
            for part in range(2):
                start = STRIP_LEN + part * QUARTER + t * LANES
                lanes = pl.ds(pl.multiple_of(start, LANES), LANES)
                strip[part, rows, :] = pieces[nq, :, lanes].astype(jnp.float32)
        return carry

    lax.fori_loop(0, BLOCKS, strip_block, 0, unroll=4)
    for layer in range(LAYERS):

        def phase_block(t, carry, layer=layer):
            for nq in range(LAYERS):
                lanes = pl.ds(pl.multiple_of(nq * QUARTER + t * LANES, LANES), LANES)
                cosine, sine = phase_parts(pieces[layer, :, lanes].astype(jnp.float32))
                rows = pl.ds(
                    pl.multiple_of(layer * PHASE_ROWS + (nq * BLOCKS + t) * COL_PITCH, 8), COLS
                )
                phases[0, rows, :] = cosine
                phases[1, rows, :] = sine
            return carry

        lax.fori_loop(0, BLOCKS, phase_block, 0, unroll=8)
        pltpu.make_async_copy(
            valid_rows(phases, layer), layer_rows(phases_out, layer), sems.at[layer]
        ).start()

    def first_block(pair, carry):
        c = pair * 2
        columns = []
        for h in range(2):
            rows = pl.ds(c + h, SUB_ROWS, stride=COL_PITCH)
            columns.append((strip[0, rows, :], strip[1, rows, :]))
        for layer in range(LAYERS):
            data = []
            for h, (real, imag) in enumerate(columns):
                turn = pl.ds(layer * PHASE_ROWS + c + h, SUB_ROWS, stride=COL_PITCH)
                cosine, sine = phases[0, turn, :], phases[1, turn, :]
                data.append(
                    jnp.concatenate(
                        [real * cosine - imag * sine, real * sine + imag * cosine], axis=0
                    )
                )
            data = jnp.concatenate(data, axis=1).astype(jnp.bfloat16)
            mixed = jnp.dot(table, data, preferred_element_type=jnp.float32)
            for h in range(2):
                real = mixed[:SUB_ROWS, h * LANES : (h + 1) * LANES]
                imag = mixed[SUB_ROWS:, h * LANES : (h + 1) * LANES]
                rows = pl.ds(layer * COLS + c + h, SUB_ROWS, stride=LINE_PITCH)
                half[0, rows, :] = real * twist_real[...] - imag * twist_imag[...]
                half[1, rows, :] = real * twist_imag[...] + imag * twist_real[...]
        return carry

    lax.fori_loop(0, COLS // 2, first_block, 0, unroll=2)

    weights = second[...]

    def second_block(pair, carry):
        data = []
        for h in range(2):
            rows = pl.ds(pl.multiple_of((pair * 2 + h) * LINE_PITCH, 8), STRIP_COLS)
            data.append(jnp.concatenate([half[0, rows, :], half[1, rows, :]], axis=1))
        data = jnp.concatenate(data, axis=0).astype(jnp.bfloat16)
        spectrum = jnp.dot(data, weights, preferred_element_type=jnp.float32)
        blocks = []
        for h in range(2):
            real = spectrum[h * STRIP_COLS : (h + 1) * STRIP_COLS, :LANES]
            imag = spectrum[h * STRIP_COLS : (h + 1) * STRIP_COLS, LANES:]
            fr = factor_real[pl.ds(pair * 2 + h, 1), :]
            fi = factor_imag[pl.ds(pair * 2 + h, 1), :]
            turned = jnp.concatenate([real * fr - imag * fi, real * fi + imag * fr], axis=0).T
            blocks.append(turned.reshape(CORE * ZX, Y, LANES))
        both = jnp.concatenate(blocks, axis=1).astype(jnp.bfloat16)
        place = pl.ds(pl.multiple_of(pair * 2 * Y, 2 * Y), 2 * Y)
        mine_ref[:, place, :] = both[:ZX]
        other_ref[:, place, :] = both[ZX:]
        return carry

    lax.fori_loop(0, SUB_ROWS // 2, second_block, 0, unroll=16)
    for layer in range(LAYERS):
        pltpu.make_async_copy(
            valid_rows(phases, layer), layer_rows(phases_out, layer), sems.at[layer]
        ).wait()


def pack_kernel(pieces, table, out_ref, total):
    total[: SUB_ROWS * Y, :] = jnp.sum(pieces[...].astype(jnp.float32), axis=0)
    rows = []
    for y in range(Y):
        block = total[pl.ds(y, SUB_ROWS, stride=Y), :]
        rows.append(jnp.concatenate([block[r * 16 : (r + 1) * 16] for r in range(4)], axis=1))
    data = jnp.concatenate(rows, axis=0).astype(jnp.bfloat16)
    packed = jnp.dot(data, table[...], preferred_element_type=jnp.float32).astype(jnp.bfloat16)
    for y in range(Y):
        for layer in range(LAYERS):
            out_ref[y * LAYERS + layer] = packed[
                y * 16 : (y + 1) * 16, layer * LANES : (layer + 1) * LANES
            ]


def subgrid_kernel(line, out_ref):
    sums = [
        sum(line[y * LAYERS + quarter].astype(jnp.float32) for y in range(Y))
        for quarter in range(LAYERS)
    ]
    for r in range(4):
        parts = []
        for p in range(2):
            for quarter in range(LAYERS):
                start = r * 2 * COLS + p * COLS
                parts.append(sums[quarter][:, start : start + COLS])
        out_ref[r * 16 : (r + 1) * 16, :] = jnp.concatenate(parts, axis=1)


def unpack_kernel(line, table, out_ref, total):
    data = jnp.concatenate(
        [
            jnp.concatenate([line[y * LAYERS + layer] for layer in range(LAYERS)], axis=1)
            for y in range(Y)
        ],
        axis=0,
    )
    grids = lax.dot_general(
        data, table[...], (((1,), (1,)), ((), ())), preferred_element_type=jnp.float32
    )
    for y in range(Y):
        for r in range(4):
            total[pl.ds(r * 16 * Y + y, 16, stride=Y), :] = grids[
                y * 16 : (y + 1) * 16, r * LANES : (r + 1) * LANES
            ]
    block = total[: SUB_ROWS * Y, :].astype(jnp.bfloat16)
    for copy in range(ZX):
        out_ref[copy] = block


def backward_kernel(
    mine, other, phases_in, twist_real, twist_imag, first, second, factor_real, factor_imag,
    out_ref, phases, half, total, sems,
):
    for layer in range(LAYERS):
        pltpu.make_async_copy(
            layer_rows(phases_in, layer), valid_rows(phases, layer), sems.at[layer]
        ).start()
    weights = second[...]

    def second_block(pair, carry):
        place = pl.ds(pl.multiple_of(pair * 2 * Y, 2 * Y), 2 * Y)
        both = jnp.concatenate([mine[:, place, :], other[:, place, :]], axis=0).astype(jnp.float32)
        data = []
        for h in range(2):
            turned = both[:, h * Y : (h + 1) * Y, :].reshape(SUBGRIDS, LANES).T
            real = turned[:STRIP_COLS]
            imag = turned[STRIP_COLS:]
            fr = factor_real[pl.ds(pair * 2 + h, 1), :]
            fi = factor_imag[pl.ds(pair * 2 + h, 1), :]
            data.append(
                jnp.concatenate([real * fr + imag * fi, imag * fr - real * fi], axis=1)
            )
        data = jnp.concatenate(data, axis=0).astype(jnp.bfloat16)
        mixed = jnp.dot(data, weights, preferred_element_type=jnp.float32)
        for h in range(2):
            real = mixed[h * STRIP_COLS : (h + 1) * STRIP_COLS, :LANES]
            imag = mixed[h * STRIP_COLS : (h + 1) * STRIP_COLS, LANES:]
            tr = twist_real[pl.ds(pair * 2 + h, 1), :]
            ti = twist_imag[pl.ds(pair * 2 + h, 1), :]
            rows = pl.ds(pair * 2 + h, STRIP_COLS, stride=LINE_PITCH)
            half[0, rows, :] = real * tr + imag * ti
            half[1, rows, :] = imag * tr - real * ti
        return carry

    lax.fori_loop(0, SUB_ROWS // 2, second_block, 0, unroll=16)

    for layer in range(LAYERS):
        pltpu.make_async_copy(
            layer_rows(phases_in, layer), valid_rows(phases, layer), sems.at[layer]
        ).wait()
    table = first[...]

    def first_block(pair, carry):
        c = pair * 2
        sums = [None] * 4
        for j in range(LAYERS):

            def column(part, h, j=j):
                start = (j * COLS + c + h) * LINE_PITCH
                return half[part, pl.ds(pl.multiple_of(start, 8), SUB_ROWS), :]

            data = jnp.concatenate(
                [
                    jnp.concatenate([column(0, 0), column(1, 0)], axis=0),
                    jnp.concatenate([column(0, 1), column(1, 1)], axis=0),
                ],
                axis=1,
            ).astype(jnp.bfloat16)
            image = jnp.dot(table, data, preferred_element_type=jnp.float32)
            for h in range(2):
                real = image[:SUB_ROWS, h * LANES : (h + 1) * LANES]
                imag = image[SUB_ROWS:, h * LANES : (h + 1) * LANES]
                rows = pl.ds(j * PHASE_ROWS + c + h, SUB_ROWS, stride=COL_PITCH)
                cosine = phases[0, rows, :]
                sine = phases[1, rows, :]
                for part, term in enumerate(
                    (real * cosine + imag * sine, imag * cosine - real * sine)
                ):
                    place = 2 * h + part
                    sums[place] = term if j == 0 else sums[place] + term
        for h in range(2):
            for part in range(2):
                total[part, pl.ds(c + h, SUB_ROWS, stride=COL_PITCH), :] = back_gain * sums[2 * h + part]
        return carry

    lax.fori_loop(0, COLS // 2, first_block, 0, unroll=8)

    def leave_block(t, carry):
        lanes = pl.ds(pl.multiple_of(t * LANES, LANES), LANES)
        for nq in range(LAYERS):
            rows = pl.ds(pl.multiple_of((nq * BLOCKS + t) * COL_PITCH, 8), COLS)
            for part in range(2):
                out_ref[nq, part, :, lanes] = total[part, rows, :].astype(jnp.bfloat16)
        return carry

    lax.fori_loop(0, BLOCKS, leave_block, 0, unroll=2)


def join_kernel(terms, out_ref, total, sems):
    def departure(cq):
        rows = pl.ds(cq * COLS, COLS)
        return pltpu.make_async_copy(total.at[cq], out_ref.at[:, rows, :], sems.at[cq])

    for cq in range(LAYERS):
        total[cq] = terms[cq].astype(jnp.float32)
        departure(cq).start()
    for cq in range(LAYERS):
        departure(cq).wait()


def on_core(kernel, name, out_shape, scratch, inputs, far_in=(), far_out=()):
    near, far = pl.BlockSpec(memory_space=pltpu.VMEM), pl.BlockSpec(memory_space=pltpu.HBM)
    return pl.pallas_call(
        kernel,
        name=name,
        out_shape=out_shape,
        in_specs=[far if i in far_in else near for i in range(inputs)],
        out_specs=[far if i in far_out else near for i in range(len(out_shape))],
        scratch_shapes=list(scratch),
        compiler_params=pltpu.CompilerParams(vmem_limit_bytes=VMEM_LIMIT),
    )


def shaped(shape, kind):
    return jax.ShapeDtypeStruct(shape, kind)


def far(values):
    return pltpu.with_memory_space_constraint(values, pltpu.HBM)


def gather(strip, screen):
    blocks = (LAYERS, COLS, STRIP_LEN + 2 * QUARTER)
    return on_core(
        gather_kernel,
        "gather",
        [pltpu.HBM(blocks, jnp.bfloat16)],
        (
            pltpu.VMEM(blocks, jnp.bfloat16),
            pltpu.SemaphoreType.DMA((LAYERS, 3)),
            pltpu.SemaphoreType.DMA((LAYERS,)),
        ),
        2,
        (0, 1),
        (0,),
    )(far(strip), far(screen))[0]


def forward(pieces, factor_real, factor_imag, second):
    blocks = shaped((ZX, SUB_ROWS * Y, LANES), jnp.bfloat16)
    phases = (2, LAYERS * SUB_ROWS, COLS, LANES)
    twist_real, twist_imag = twiddle()
    return on_core(
        forward_kernel,
        "ahead",
        [blocks, blocks, pltpu.HBM(phases, jnp.float32)],
        (
            pltpu.VMEM((2, LAYERS * PHASE_ROWS + COL_PITCH, LANES), jnp.float32),
            pltpu.VMEM((2, PHASE_ROWS + COL_PITCH, LANES), jnp.float32),
            pltpu.VMEM((2, (SUB_ROWS + 1) * LINE_PITCH, LANES), jnp.float32),
            pltpu.SemaphoreType.DMA((LAYERS,)),
        ),
        7,
        far_out=(2,),
    )(pieces, twist_real, twist_imag, first_tables()[0], second, factor_real, factor_imag)


def backward(mine, other, phases, factor_real, factor_imag, second):
    twist_real, twist_imag = twiddle()
    return on_core(
        backward_kernel,
        "back",
        [shaped((LAYERS, 2, COLS, QUARTER), jnp.bfloat16)],
        (
            pltpu.VMEM((2, LAYERS * PHASE_ROWS + COL_PITCH, LANES), jnp.float32),
            pltpu.VMEM((2, (STRIP_COLS + 1) * LINE_PITCH, LANES), jnp.float32),
            pltpu.VMEM((2, PHASE_ROWS + COL_PITCH, LANES), jnp.float32),
            pltpu.SemaphoreType.DMA((LAYERS,)),
        ),
        9,
        far_in=(2,),
    )(
        mine, other, far(phases), twist_real, twist_imag, first_tables()[1], second,
        factor_real, factor_imag,
    )[0]


def spread(cell_index, length, kernel_taps):
    tap_count = kernel_taps.shape[0]
    offset = (jnp.arange(length, dtype=jnp.int32)[None, :] - cell_index[:, None]) % length
    wanted = (jnp.arange(tap_count, dtype=jnp.int32) - tap_count // 2) % length
    matches = (offset[:, :, None] == wanted[None, None, :]).astype(jnp.float32)
    return jnp.sum(matches * kernel_taps, axis=2)


def prepare(row_cells, column_cells, plane, angle_table, kernel_taps):
    row_weights = spread(row_cells, SUB_ROWS, kernel_taps)
    column_weights = spread(column_cells, STRIP_COLS, kernel_taps)
    plane_pick = (plane[:, None] == jnp.arange(PLANES, dtype=jnp.int32)[None, :]).astype(
        jnp.float32
    )
    phase_angle = jnp.sum(plane_pick * angle_table[None, :], axis=1)
    return (row_weights, column_weights, jnp.cos(phase_angle), jnp.sin(phase_angle))


def degrid(subgrid, observed_vis, row_weights, column_weights, cosine, sine_part):
    kernel_rows = jnp.dot(row_weights, subgrid, precision=lax.Precision.HIGHEST)
    model_real = jnp.sum(kernel_rows[:, :STRIP_COLS] * column_weights, axis=1)
    model_imag = jnp.sum(kernel_rows[:, STRIP_COLS:] * column_weights, axis=1)
    residual_real = observed_vis[0] - (model_real * cosine - model_imag * sine_part)
    residual_imag = observed_vis[1] - (model_real * sine_part + model_imag * cosine)
    weighted_real = residual_real * cosine + residual_imag * sine_part
    weighted_imag = residual_imag * cosine - residual_real * sine_part
    spread_cols = jnp.concatenate(
        [weighted_real[:, None] * column_weights, weighted_imag[:, None] * column_weights], axis=1
    )
    adjoint = jnp.dot(row_weights.T, spread_cols, precision=lax.Precision.HIGHEST)
    return ((residual_real, residual_imag), adjoint)


def exchange(blocks, axes, groups=None):
    return lax.all_to_all(
        blocks, axes, split_axis=0, concat_axis=0, tiled=True, axis_index_groups=groups
    )


def local(
    model_strip,
    screen_angle,
    facet_window,
    facet_shift,
    kernel_taps,
    plane_angle,
    u_cell,
    v_cell,
    w_plane,
    observed,
):
    swapped = lax.axis_index("facet") % CORE == 1

    pieces = exchange(gather(model_strip[0], screen_angle[0, 0]), "layer")

    factor_real, factor_imag = facet_factor(facet_window[0], facet_shift[0], swapped)
    plain = second_tables(STAGE_ORDER)
    crossed = second_tables(np.roll(STAGE_ORDER, SUBGRIDS // CORE))
    second_ahead = jnp.where(swapped, crossed[0], plain[0])
    second_back = jnp.where(swapped, crossed[1], plain[1])
    prepared = prepare(u_cell[0, 0], v_cell[0, 0], w_plane[0, 0], plane_angle[0], kernel_taps)
    observed_vis = (observed[0, 0, 0], observed[0, 0, 1])
    (
        pieces, factor_real, factor_imag, second_ahead, second_back, prepared, observed_vis
    ) = lax.optimization_barrier(
        (pieces, factor_real, factor_imag, second_ahead, second_back, prepared, observed_vis)
    )
    mine, other, phases = forward(pieces, factor_real, factor_imag, second_ahead)

    arrived = lax.ppermute(other, "facet", CORE_SWAP)
    pair_sum = (mine.astype(jnp.float32) + arrived.astype(jnp.float32)).astype(jnp.bfloat16)
    plane_terms = exchange(pair_sum, "facet", PLANE_GROUPS)
    table = pack_table()
    piece = (SUB_ROWS // 4, 2 * STRIP_COLS)
    packed = on_core(
        pack_kernel,
        "pack",
        [shaped((Y * LAYERS, *piece), jnp.bfloat16)],
        (pltpu.VMEM((SUB_ROWS * Y + Y, LANES), jnp.float32),),
        2,
    )(plane_terms, table)[0]
    subgrid = on_core(
        subgrid_kernel, "subgrid", [shaped((SUB_ROWS, 2 * STRIP_COLS), jnp.float32)], (), 1
    )(exchange(packed, ("layer", "facet"), LINE_GROUPS))[0]

    residual, adjoint = degrid(subgrid, observed_vis, *prepared)
    residual, adjoint = lax.optimization_barrier((residual, adjoint.astype(jnp.bfloat16)))

    sent = (
        adjoint.reshape(4, SUB_ROWS // 4, 2, LAYERS, COLS)
        .transpose(3, 1, 0, 2, 4)
        .reshape(1, LAYERS, *piece)
    )
    line = exchange(
        jnp.broadcast_to(sent, (Y, LAYERS, *piece)).reshape(Y * LAYERS, *piece),
        ("layer", "facet"),
        LINE_GROUPS,
    )
    copies = on_core(
        unpack_kernel,
        "unpack",
        [shaped((ZX, SUB_ROWS * Y, LANES), jnp.bfloat16)],
        (pltpu.VMEM((SUB_ROWS * Y + Y, LANES), jnp.float32),),
        2,
    )(line, table)[0]
    mine_grids = exchange(copies, "facet", PLANE_GROUPS)
    mine_grids, residual = lax.optimization_barrier((mine_grids, residual))
    other_grids = lax.ppermute(mine_grids, "facet", CORE_SWAP)
    other_grids, residual = lax.optimization_barrier((other_grids, jnp.stack(residual)))
    leaving = backward(mine_grids, other_grids, phases, factor_real, factor_imag, second_back)
    gradient = on_core(
        join_kernel,
        "join",
        [pltpu.HBM((2, STRIP_COLS, QUARTER), jnp.float32)],
        (
            pltpu.VMEM((LAYERS, 2, COLS, QUARTER), jnp.float32),
            pltpu.SemaphoreType.DMA((LAYERS,)),
        ),
        1,
        far_out=(0,),
    )(exchange(leaving, "layer"))[0]
    return (residual[None, None], gradient[None])


def solution(mesh):
    return jax.shard_map(
        local,
        mesh=mesh,
        in_specs=(
            P("facet", None, None, "layer"),
            P("layer", "facet", None, None),
            P("facet", None),
            P("facet"),
            P(),
            P("layer", None),
            P("layer", "facet", None),
            P("layer", "facet", None),
            P("layer", "facet", None),
            P("layer", "facet", None, None),
        ),
        out_specs=(P("layer", "facet", None, None), P("facet", None, None, "layer")),
        check_vma=False,
    )
```
